32 devices in a mesh: tiles: 2 (over y), disp: 4 (over z), rows: 2 (over x), cols: 2 (over core).
Axes of the slice: x: 2, y: 2, z: 4, core: 2. Of those that a mesh axis runs over, the one named last changes fastest.
Arguments:
- left_feat: bfloat16 [4, 256, 320], P(('tiles', 'rows'), ('cols', 'disp')), parts along dimension 0, may hold values from -64 to 64
- right_feat: bfloat16 [4, 256, 320], P(('tiles', 'rows'), ('cols', 'disp')), parts along dimension 0, may hold values from -64 to 64
- conv_first: bfloat16 [27, 32, 40], replicated, may hold values from -0.1875 to 0.1875
- conv_mid: bfloat16 [2, 27, 32, 32], replicated, may hold values from -0.21875 to 0.21875
- conv_last: bfloat16 [27, 1, 32], replicated, may hold values from -3 to 3
Outputs:
- estimate: float32 [4, 256], P(('tiles', 'rows'), ('cols', 'disp')), parts along dimension 0
The draws below stay inside these ranges and needn't reach their ends.
There are 2 independent parts, one for each index of `tiles`. The reference program is written for one: setup_inputs(seed, part) draws one part's arguments, and reference() takes and returns one part's arrays. A program takes and returns all parts, laid end to end along the dimension named above; an argument that names none is the same for every part. Nothing has to cross between parts.
All inputs are finite; a program needn't handle non-finite values.
Results may differ from the reference program's by a relative error of at most 0.012.
The reference program's roundings to bfloat16 on the way (of `volume`) count: a program that leaves them out, or rounds other values in their place, can miss the bound.
Values may be sent and summed in bfloat16 or wider, within the bound.
A program may use at most 64 MiB of HBM per device.

```python
import jax
import jax.numpy as jnp
from jax import lax

C = 320
G = 40
F = 32
MID = 2
DISP = 64
H = 2
W = 256


def boost_rows(key):
    base = jax.random.fold_in(key, 7)
    pick_key, mask_key, level_key = jax.random.split(base, 3)
    pick = jax.random.randint(pick_key, (), 0, H)
    chosen = (jax.random.randint(mask_key, (H,), 0, 8) == 0) | (jnp.arange(H) == pick)
    levels = jnp.array([7.0, 9.0, 11.0], jnp.float32)[jax.random.randint(level_key, (H,), 0, 3)]
    return jnp.where(chosen, levels, 1.0).astype(jnp.float32)[:, None, None]


def draw_features(key, salt):
    boost = boost_rows(key)
    own_key = jax.random.fold_in(key, salt)
    first_key = jax.random.fold_in(own_key, 0)
    values = jnp.clip(jax.random.normal(first_key, (H, W, C), jnp.float32), -4.0, 4.0)
    values = values * boost
    return values.astype(jnp.bfloat16)


def draw_left_feat(key, part):
    return draw_features(key, 11)


def draw_right_feat(key, part):
    return draw_features(key, 12)


def noise(key, extent, deviation, limit, held_as=jnp.bfloat16):
    result = deviation * jax.random.normal(key, extent, jnp.float32)
    return jnp.clip(result, min=-limit, max=limit).astype(held_as)


def setup_inputs(seed: int = 0, part: int = 0) -> dict:
    streams_of = jax.random.split(jax.random.key(seed), 6)
    part_splits = jax.random.split(jax.random.fold_in(streams_of[5], part), 6)
    return {
        "left_feat": draw_left_feat(jax.random.fold_in(jax.random.fold_in(streams_of[5], part), 71), part),
        "right_feat": draw_right_feat(jax.random.fold_in(jax.random.fold_in(streams_of[5], part), 71), part),
        "conv_first": noise(streams_of[2], (27, F, G), (27 * G) ** -0.5, 0.1875),
        "conv_mid": noise(streams_of[3], (MID, 27, F, F), (27 * F) ** -0.5, 0.21875),
        "conv_last": noise(streams_of[4], (27, 1, F), 0.5, 3.0),
    }


def conv_layer(inputs, kernel):
    taps = jnp.transpose(kernel, (1, 2, 0)).reshape(kernel.shape[1], kernel.shape[2], 3, 3, 3).astype(jnp.float32)
    planes = jnp.transpose(inputs, (1, 0, 2, 3))[None].astype(jnp.float32)
    output = lax.conv_general_dilated(planes, taps, (1, 1, 1), ((1, 1), (1, 1), (1, 1)), dimension_numbers=("NCDHW", "OIDHW", "NCDHW"), precision=lax.Precision.HIGHEST)
    return jnp.transpose(output[0], (1, 0, 2, 3))


def reference(left_feat, right_feat, conv_first, conv_mid, conv_last):
    group_size = C // G
    padded_right = jnp.pad(right_feat, ((0, 0), (DISP, 0), (0, 0)))
    left_groups = left_feat.astype(jnp.float32).reshape(H, W, G, group_size)

    def single(disp_value):
        shifted = lax.dynamic_slice_in_dim(padded_right, (DISP - disp_value).astype(jnp.int32), W, 1)
        right_groups = shifted.astype(jnp.float32).reshape(H, W, G, group_size)
        corr = jnp.sum(left_groups * right_groups, axis=3) / group_size
        return jnp.transpose(corr, (2, 0, 1)).astype(jnp.bfloat16)

    volume = lax.map(single, jnp.arange(DISP, dtype=jnp.int32))
    hidden = jax.nn.relu(conv_layer(volume, conv_first))
    for layer in range(MID):
        hidden = jax.nn.relu(conv_layer(hidden, conv_mid[layer]))
    cost_cube = conv_layer(hidden, conv_last)[:, 0]
    highest = jnp.max(cost_cube, axis=0)
    weights = jnp.exp(cost_cube - highest[None])
    levels = (jnp.arange(DISP, dtype=jnp.float32) / DISP)[:, None, None]
    return jnp.sum(weights * levels, axis=0) / jnp.sum(weights, axis=0)
```

```python
import functools

import jax
import jax.numpy as jnp
from jax import lax
from jax.experimental import pallas as pl
from jax.experimental.pallas import tpu as pltpu
from jax.sharding import PartitionSpec as P

MID = 2
DDEV = 16


def extended_2(block, sides, width):
    for axis, dim in sides:
        count = lax.axis_size(axis)
        forward = [(i, i + 1) for i in range(count - 1)]
        backward = [(target, source) for source, target in forward]
        low = lax.ppermute(
            lax.slice_in_dim(block, block.shape[dim] - width, None, axis=dim), axis, forward
        )
        high = lax.ppermute(lax.slice_in_dim(block, 0, width, axis=dim), axis, backward)
        block = jnp.concatenate([low, block, high], axis=dim)
    return block


def passed_along(x, axis, by):
    peers = lax.axis_size(axis)
    pairs = [(i, i + by) for i in range(peers) if 0 <= i + by < peers]
    return lax.ppermute(x, axis, pairs)


def combined_all(part, axis, combine):
    gathered = jax.tree.map(lambda a: lax.all_gather(a, axis), part)

    def take(source):
        return jax.tree.map(lambda a: lax.dynamic_index_in_dim(a, source, 0, False), gathered)

    return lax.fori_loop(
        1, lax.axis_size(axis), lambda source, state: combine(state, take(source)), take(0)
    )


def correlate(left_full, extended, groups, first_disp, count, total_disp):
    rows_here, width_here, channels = left_full.shape
    group_size = channels // groups
    left_groups = left_full.reshape(rows_here, width_here, groups, group_size)

    def single(offset):
        disp_value = first_disp + offset
        shifted = lax.dynamic_slice_in_dim(extended, 2 * width_here - disp_value, width_here, 1)
        right_groups = shifted.reshape(rows_here, width_here, groups, group_size)
        corr = (
            jnp.einsum(
                "hwgc,hwgc->ghw", left_groups, right_groups, preferred_element_type=jnp.float32
            )
            / group_size
        )
        inside = (disp_value >= 0) & (disp_value < total_disp)
        return jnp.where(inside, corr, 0.0).astype(jnp.bfloat16)

    return lax.map(single, jnp.arange(count, dtype=jnp.int32))


def convolve(padded, kernel):
    depth_out = padded.shape[0] - 2
    in_chans = padded.shape[1]
    rows_out = padded.shape[2] - 2
    cols_out = padded.shape[3] - 2
    out_chans = kernel.shape[1]
    columns = jnp.concatenate(
        [
            padded[:, :, row_tap : row_tap + rows_out, col_tap : col_tap + cols_out]
            for row_tap in range(3)
            for col_tap in range(3)
        ],
        axis=1,
    )
    flat = columns.reshape(depth_out + 2, 9 * in_chans, rows_out * cols_out)
    summed = jnp.zeros((depth_out, out_chans, rows_out * cols_out), jnp.float32)
    for disp_tap in range(3):
        taps = (
            jnp.transpose(kernel[9 * disp_tap : 9 * disp_tap + 9], (1, 0, 2))
            .reshape(out_chans, 9 * in_chans)
            .astype(flat.dtype)
        )
        summed = summed + jnp.einsum(
            "ok,dkn->don",
            taps,
            flat[disp_tap : disp_tap + depth_out],
            preferred_element_type=jnp.float32,
            precision=lax.Precision.HIGHEST,
        )
    return summed.reshape(depth_out, out_chans, rows_out, cols_out)


def widen(hidden):
    return extended_2(hidden, (("disp", 0), ("rows", 2), ("cols", 3)), 1)


def combine_parts(earlier, later):
    highest = jnp.maximum(earlier[0], later[0])
    scale_one = jnp.exp(earlier[0] - highest)
    scale_two = jnp.exp(later[0] - highest)
    return (
        highest,
        earlier[1] * scale_one + later[1] * scale_two,
        earlier[2] * scale_one + later[2] * scale_two,
    )


def shards(left_feat, right_feat, conv_first, conv_mid, conv_last):
    piece_width = left_feat.shape[1]
    groups = conv_first.shape[2]
    disp_count = lax.axis_size("disp")
    depth_here = DDEV
    total_disp = depth_here * disp_count
    first_disp = lax.axis_index("disp") * depth_here
    left_full, right_full = (
        lax.all_gather(left_feat, "disp", axis=1, tiled=True),
        lax.all_gather(right_feat, "disp", axis=1, tiled=True),
    )
    prior_full = passed_along(right_full, "cols", 1)
    extended = jnp.concatenate([jnp.zeros_like(right_full), prior_full, right_full], axis=1)
    volume = correlate(left_full, extended, groups, first_disp, depth_here, total_disp)
    padded = extended_2(volume, (("disp", 0), ("rows", 2), ("cols", 3)), 1)
    hidden = jax.nn.relu(convolve(padded, conv_first))
    for layer in range(MID):
        hidden = jax.nn.relu(convolve(widen(hidden), conv_mid[layer]))
    cost_cube = convolve(widen(hidden), conv_last)[:, 0]
    levels = (
        (first_disp + jnp.arange(depth_here, dtype=jnp.int32)).astype(jnp.float32) / total_disp
    )[:, None, None]
    local_high = jnp.max(cost_cube, axis=0)
    weights = jnp.exp(cost_cube - local_high[None])
    merged = combined_all(
        (local_high, jnp.sum(weights, axis=0), jnp.sum(weights * levels, axis=0)),
        "disp",
        combine_parts,
    )
    whole_row = merged[2] / merged[1]
    return lax.dynamic_slice_in_dim(whole_row, lax.axis_index("disp") * piece_width, piece_width, 1)


HALO = 4
GROUP = 4
EDGE = 16
SLAB = 128
NEAR = 8


def build_permutation(perm_ref, channels, groups):
    size = channels // groups
    rows, lanes = perm_ref.shape
    part = rows // 2
    lane = lax.broadcasted_iota(jnp.int32, (1, lanes), 1)
    group = lane % 64
    for row in range(2):
        wanted = group * size + lane // SLAB
        wanted = jnp.where((group < groups) & ((lane // 64) % 2 == row), wanted, -1)
        channel = lax.broadcasted_iota(jnp.int32, (part, lanes), 0)
        block = (channel == wanted).astype(jnp.float32).astype(jnp.bfloat16)
        perm_ref[row * part : (row + 1) * part, :] = block


def tap_of(a, r_in, r_out, e):
    return 9 * a + 3 * (r_in - r_out + 1) + e


def place_first(target, at, lead, slabs):
    for a, slab in enumerate(slabs):
        lane = SLAB * (lead + a)
        target[at : at + slab.shape[0], lane : lane + SLAB] = slab


def build_first(taps_ref, pair_ref, quad_ref):
    pair_ref[...] = jnp.zeros_like(pair_ref)
    quad_ref[...] = jnp.zeros_like(quad_ref)
    outs, ins = taps_ref.shape[1:]
    blank = jnp.zeros((outs, 64 - ins), jnp.float32)
    for e in range(3):
        for r_out in range(2):
            slabs = []
            for a in range(3):
                parts = []
                for r_in in range(2):
                    parts += [taps_ref[tap_of(a, r_in, r_out, e)].astype(jnp.float32), blank]
                slabs.append(jnp.concatenate(parts, axis=1).astype(jnp.bfloat16))
            if e < 2:
                for d_out in range(2):
                    place_first(pair_ref, e * 128 + d_out * 64 + r_out * 32, d_out, slabs)
            else:
                for d_out in range(GROUP):
                    place_first(quad_ref, d_out * 64 + r_out * 32, d_out, slabs)


def place_mid(target, at, lead, block):
    for half in range(2):
        piece = block[:, SLAB * half : SLAB * half + SLAB]
        for copy in range(2):
            lane = 2 * SLAB * (lead + half) + SLAB * copy
            target[at : at + piece.shape[0], lane : lane + SLAB] = piece


def build_mid(taps_ref, pair_ref, quad_ref):
    pair_ref[...] = jnp.zeros_like(pair_ref)
    quad_ref[...] = jnp.zeros_like(quad_ref)
    outs = taps_ref.shape[1]
    blank = jnp.zeros((outs, 64), jnp.float32)
    for e in range(3):
        for r_out in range(2):
            slabs = [
                taps_ref[tap_of(a, r_in, r_out, e)].astype(jnp.float32)
                for a in range(3)
                for r_in in range(2)
            ]
            shifted = (
                jnp.concatenate(slabs + [blank], axis=1).astype(jnp.bfloat16),
                jnp.concatenate([blank] + slabs, axis=1).astype(jnp.bfloat16),
            )
            if e < 2:
                for d_out in range(2):
                    place_mid(pair_ref, e * 128 + d_out * 64 + r_out * 32, 0, shifted[d_out])
            else:
                for d_out in range(GROUP):
                    place_mid(
                        quad_ref, d_out * 64 + r_out * 32, d_out // 2, shifted[d_out % 2]
                    )


def build_last(taps_ref, line_ref, row):
    taps = taps_ref[...].astype(jnp.float32)
    lines = []
    for e in range(3):
        for d_out in range(GROUP):
            parts = []
            for a in range(3):
                for r_in in range(2):
                    upper, lower = (tap_of(a, r_in, r_out, e) for r_out in range(2))
                    parts.append(
                        jnp.where(row == 0, taps[upper : upper + 1], taps[lower : lower + 1])
                    )
            if d_out > 0:
                parts.insert(0, jnp.zeros((1, 64 * d_out), jnp.float32))
            if d_out < GROUP - 1:
                parts.append(jnp.zeros((1, 64 * (GROUP - 1 - d_out)), jnp.float32))
            lines.append(jnp.concatenate(parts, axis=1))
        lines.append(jnp.zeros((8 - GROUP, 3 * SLAB), jnp.float32))
    lines.append(jnp.zeros((8, 3 * SLAB), jnp.float32))
    block = jnp.concatenate(lines, axis=0).astype(jnp.bfloat16)
    for pair in range(3):
        piece = block[:, SLAB * pair : SLAB * pair + SLAB]
        for copy in range(2):
            lane = SLAB * (2 * pair + copy)
            line_ref[:, lane : lane + SLAB] = piece


def across(x, banded):
    return lax.dot_general(
        x, banded, (((1,), (1,)), ((), ())), preferred_element_type=jnp.float32
    )


def exchange_plan(width):
    own = EDGE + 2 * width
    left_at = own + width + EDGE
    near = []
    far = []
    near.append((1, 0, 1, 0, own, width))
    near.append((0, 0, 1, 0, left_at + EDGE, width))
    for other in (1, 0):
        near.append((1, 1, other, 0, own - width, width))
        near.append((0, 1, other, width - EDGE, left_at, EDGE))
        near.append((1, -1, other, 0, own + width, EDGE))
        near.append((0, -1, other, 0, left_at + EDGE + width, EDGE))
        far.append((1, 2, other, 0, own - 2 * width, width))
        far.append((1, 3, other, width - EDGE, 0, EDGE))
    return tuple(near), tuple(far), own, left_at, left_at + width + 2 * EDGE


def exchange_steps(left_ref, right_ref, held, send_sem, recv_sem, own_sem):
    width, channels = left_ref.shape[1:]
    near, far, own, left_at, _ = exchange_plan(width)
    copies = near + far
    row, col, disp = lax.axis_index("rows"), lax.axis_index("cols"), lax.axis_index("disp")
    col_disps = lax.axis_size("disp")
    pieces = col_disps * lax.axis_size("cols")
    piece = col * col_disps + disp
    barrier = pltpu.get_barrier_semaphore()
    targets = sorted({(by, other) for _, by, other, _, _, _ in copies})

    def device(other, by):
        target = piece + by
        target_col = (target >= col_disps).astype(jnp.int32)
        return {
            "tiles": lax.axis_index("tiles"),
            "disp": target - col_disps * target_col,
            "rows": 1 - row if other else row,
            "cols": target_col,
        }

    def exists(by):
        return (piece + by >= 0) & (piece + by < pieces)

    def landing(target, count):
        return held.at[row, pl.ds(target, count)]

    def copy(number):
        view, by, other, source, target, count = copies[number]
        return pltpu.make_async_remote_copy(
            src_ref=(left_ref if view == 0 else right_ref).at[0, pl.ds(source, count)],
            dst_ref=landing(target, count),
            send_sem=send_sem.at[number],
            recv_sem=recv_sem.at[number],
            device_id=device(other, by),
            device_id_type=pl.DeviceIdType.MESH,
        )

    own_loads = [
        pltpu.make_async_copy(source.at[0], landing(target, width), own_sem.at[number])
        for number, (source, target) in enumerate(
            ((left_ref, left_at + EDGE), (right_ref, own))
        )
    ]

    def greet():
        held[...] = jnp.zeros_like(held)
        for by, other in targets:

            @pl.when(exists(-by))
            def _():
                pl.semaphore_signal(
                    barrier,
                    inc=1,
                    device_id=device(other, -by),
                    device_id_type=pl.DeviceIdType.MESH,
                )

        for load in own_loads:
            load.start()

    def send():
        partners = jnp.int32(0)
        for by, _ in targets:
            partners = partners + exists(by).astype(jnp.int32)
        pl.semaphore_wait(barrier, partners)
        for number in range(len(copies)):

            @pl.when(exists(copies[number][1]))
            def _():
                copy(number).start()

    def receive(numbers):
        for number in numbers:

            @pl.when(exists(-copies[number][1]))
            def _():
                copy(number).wait_recv()

    def receive_near():
        for load in own_loads:
            load.wait()
        receive(range(len(near)))

    def receive_far():
        receive(range(len(near), len(copies)))

    def finish():
        for number in range(len(copies)):

            @pl.when(exists(copies[number][1]))
            def _():
                copy(number).wait_send()

    return greet, send, receive_near, receive_far, finish


def whole_kernel(
    disps,
    width_all,
    left_ref,
    right_ref,
    first_hbm,
    mid_hbm,
    last_hbm,
    out_ref,
    feat_ref,
    send_sem,
    recv_sem,
    own_sem,
    load_sem,
    perm_ref,
    first_taps,
    mid_taps,
    last_taps,
    a_ref,
    p_ref,
    f_ref,
    pair_ref,
    quad_ref,
    line_ref,
):
    width_here = out_ref.shape[1]
    wide = width_here + 2 * HALO
    groups_d = disps // GROUP + 1
    channels, groups = left_ref.shape[2], first_taps.shape[2]
    size = channels // groups
    _, _, own, left_at, held_rows = exchange_plan(width_here)
    greet, send, receive_near, receive_far, finish = exchange_steps(
        left_ref, right_ref, feat_ref, send_sem, recv_sem, own_sem
    )
    loads = [
        pltpu.make_async_copy(source, target, load_sem.at[number])
        for number, (source, target) in enumerate(
            ((first_hbm, first_taps), (mid_hbm, mid_taps), (last_hbm, last_taps))
        )
    ]
    greet()
    for load in loads:
        load.start()
    send()
    build_permutation(perm_ref, channels, groups)
    a_ref[0, 0:wide, :] = jnp.zeros((wide, 6 * SLAB), jnp.bfloat16)
    for layer in range(MID + 2):
        a_ref[layer, (groups_d - 1) * wide : groups_d * wide, 4 * SLAB :] = jnp.zeros(
            (wide, 2 * SLAB), jnp.bfloat16
        )
    loads[0].wait()
    build_first(first_taps, pair_ref.at[0], quad_ref.at[0])
    loads[1].wait()
    for layer in range(MID):
        build_mid(mid_taps.at[layer], pair_ref.at[layer + 1], quad_ref.at[layer + 1])
    loads[2].wait()
    build_last(last_taps, line_ref, lax.axis_index("rows"))

    def permute(start, stop):
        for at in range(0, size * SLAB, 2 * SLAB):
            lanes = slice(at, at + 2 * SLAB)
            both = jnp.dot(
                feat_ref[0, start:stop],
                perm_ref[0:channels, lanes],
                preferred_element_type=jnp.float32,
            ) + jnp.dot(
                feat_ref[1, start:stop],
                perm_ref[channels : 2 * channels, lanes],
                preferred_element_type=jnp.float32,
            )
            f_ref[at // SLAB, start:stop] = both[:, :SLAB]
            f_ref[at // SLAB + 1, start:stop] = both[:, SLAB:]

    def volume(start, stop):
        for group in range(start, stop):
            sums = [None] * GROUP
            for k in range(size):
                left = f_ref[k, left_at + EDGE - HALO : left_at + EDGE - HALO + wide]
                for place in range(GROUP):
                    at = own - HALO - (GROUP * (group - 1) + place)
                    term = left * f_ref[k, at : at + wide]
                    sums[place] = term if k == 0 else sums[place] + term
            for place in range(GROUP):
                slab = (sums[place] / size).astype(jnp.bfloat16)
                here = slice(group * wide, (group + 1) * wide)
                a_ref[0, here, SLAB * place : SLAB * place + SLAB] = slab
                if place < 2:
                    before = slice((group - 1) * wide, group * wide)
                    lane = SLAB * (GROUP + place)
                    a_ref[0, before, lane : lane + SLAB] = slab

    piece = lax.axis_index("cols") * lax.axis_size("disp") + lax.axis_index("disp")
    column = piece * width_here - HALO + lax.broadcasted_iota(jnp.int32, (wide, SLAB), 0)
    in_image = (column >= 0) & (column < width_all)
    lane_disp = lax.broadcasted_iota(jnp.int32, (wide, SLAB), 1) // 64

    def convolve_groups(layer, start, stop):
        source, target, part = a_ref.at[layer], a_ref.at[layer + 1], p_ref.at[layer]
        middle = (start + stop) // 2

        def multiply(slab, first, last, lanes, taps_ref):
            rows = slice(first * wide, last * wide)
            got = across(source[rows, lanes], taps_ref[layer])
            held = slice(8 + first * wide, 8 + last * wide)
            part[slab, held] = got[:, :SLAB]
            part[slab + 1, held] = got[:, SLAB:]

        multiply(0, start, stop, slice(0, 4 * SLAB), pair_ref)
        multiply(2, start, stop, slice(2 * SLAB, 6 * SLAB), pair_ref)
        multiply(4, start, middle, slice(0, 6 * SLAB), quad_ref)
        multiply(4, middle, stop, slice(0, 6 * SLAB), quad_ref)
        base = layer + 1 - HALO
        for group in range(start, stop):
            at = 8 + group * wide
            here = slice(group * wide, (group + 1) * wide)
            before = slice((group - 1) * wide, group * wide)
            for half in range(2):
                total = (
                    part[2 * half, at - 1 : at - 1 + wide]
                    + part[2 * half + 1, at : at + wide]
                    + part[4 + half, at + 1 : at + 1 + wide]
                )
                low = base + GROUP * group + 2 * half
                keep = in_image
                if low < 0 or low + 2 > disps:
                    keep = keep & (lane_disp >= -low) & (lane_disp < disps - low)
                total = jnp.where(keep, jnp.maximum(total, 0.0), 0.0)
                high = total.astype(jnp.bfloat16)
                rest = (total - high.astype(jnp.float32)).astype(jnp.bfloat16)
                lane = 2 * SLAB * half
                target[here, lane : lane + SLAB] = high
                target[here, lane + SLAB : lane + 2 * SLAB] = rest
                if half == 0 and group > 0:
                    target[before, 4 * SLAB : 5 * SLAB] = high
                    target[before, 5 * SLAB : 6 * SLAB] = rest

    receive_near()
    receive_far()
    permute(0, held_rows)
    volume(1, groups_d)
    for layer in range(MID + 1):
        convolve_groups(layer, 0, groups_d)

    per = SLAB // wide
    lane = lax.broadcasted_iota(jnp.int32, (8, SLAB), 1)
    place = lax.broadcasted_iota(jnp.int32, (8, SLAB), 0)
    within = lane // wide
    costs = []
    valids = []
    for first in range(0, groups_d - 1, per):
        taken = a_ref[MID + 1, first * wide : first * wide + SLAB]
        parts = across(line_ref[...], taken)
        cost = (
            pltpu.roll(parts[0:8], 1, 1) + parts[8:16] + pltpu.roll(parts[16:24], SLAB - 1, 1)
        )
        valid = (place < GROUP) & (within < min(per, groups_d - 1 - first))
        valids.append(valid)
        costs.append(jnp.where(valid, cost, -jnp.inf))
    def gathered(x, combine):
        return functools.reduce(
            combine, [x] + [pltpu.roll(x, SLAB - wide * k, 1) for k in range(1, per)]
        )

    top = jnp.max(functools.reduce(jnp.maximum, costs), axis=0, keepdims=True)
    top = gathered(jnp.broadcast_to(top, (8, SLAB)), jnp.maximum)
    tops = top
    for k in range(1, per):
        tops = jnp.where(within == k, pltpu.roll(top, wide * k, 1), tops)
    weight_sum = jnp.zeros((8, SLAB), jnp.float32)
    level_sum = jnp.zeros((8, SLAB), jnp.float32)
    for number, cost in enumerate(costs):
        weight = jnp.where(valids[number], jnp.exp(cost - tops), 0.0)
        level = GROUP * (number * per + within) + place
        weight_sum += weight
        level_sum += weight * (level.astype(jnp.float32) * (1.0 / disps))
    weight_sum = gathered(jnp.broadcast_to(jnp.sum(weight_sum, axis=0, keepdims=True), (8, SLAB)), jnp.add)
    level_sum = gathered(jnp.broadcast_to(jnp.sum(level_sum, axis=0, keepdims=True), (8, SLAB)), jnp.add)
    line = pltpu.roll(level_sum / weight_sum, SLAB - HALO, 1)
    out_ref[...] = line[0:1, 0:width_here]
    finish()


def window_shards(left_feat, right_feat, conv_first, conv_mid, conv_last):
    width = left_feat.shape[1]
    channels = left_feat.shape[2]
    groups = conv_first.shape[2]
    disps = DDEV * lax.axis_size("disp")
    width_all = width * lax.axis_size("disp") * lax.axis_size("cols")
    near, far, _, _, held_rows = exchange_plan(width)
    count = len(near) + len(far)
    wide = width + 2 * HALO
    rows = (disps // GROUP + 1) * wide
    size = channels // groups
    return pl.pallas_call(
        functools.partial(whole_kernel, disps, width_all),
        out_shape=jax.ShapeDtypeStruct((1, width), jnp.float32),
        in_specs=[pl.BlockSpec(memory_space=pltpu.HBM)] * 5,
        out_specs=pl.BlockSpec(memory_space=pltpu.VMEM),
        scratch_shapes=[
            pltpu.VMEM((2, held_rows, channels), jnp.bfloat16),
            pltpu.SemaphoreType.DMA((count,)),
            pltpu.SemaphoreType.DMA((count,)),
            pltpu.SemaphoreType.DMA((2,)),
            pltpu.SemaphoreType.DMA((3,)),
            pltpu.VMEM((2 * channels, size * SLAB), jnp.bfloat16),
            pltpu.VMEM(conv_first.shape, jnp.bfloat16),
            pltpu.VMEM(conv_mid.shape, jnp.bfloat16),
            pltpu.VMEM((27, conv_last.shape[2]), jnp.bfloat16),
            pltpu.VMEM((MID + 2, rows + 2 * wide, 6 * SLAB), jnp.bfloat16),
            pltpu.VMEM((MID + 1, 6, rows + 16, SLAB), jnp.float32),
            pltpu.VMEM((size, held_rows, SLAB), jnp.float32),
            pltpu.VMEM((MID + 1, 2 * SLAB, 4 * SLAB), jnp.bfloat16),
            pltpu.VMEM((MID + 1, 2 * SLAB, 6 * SLAB), jnp.bfloat16),
            pltpu.VMEM((32, 6 * SLAB), jnp.bfloat16),
        ],
        compiler_params=pltpu.CompilerParams(
            vmem_limit_bytes=56 * 1024 * 1024, collective_id=0, has_side_effects=True
        ),
    )(left_feat, right_feat, conv_first, conv_mid, conv_last.reshape(27, -1))


def solution(mesh):
    rows, pieces = mesh.shape["rows"], mesh.shape["cols"] * mesh.shape["disp"]
    body = window_shards if rows == 2 and mesh.shape["disp"] == 4 and pieces == 8 else shards
    return jax.shard_map(
        body,
        mesh=mesh,
        in_specs=(
            P(("tiles", "rows"), ("cols", "disp"), None),
            P(("tiles", "rows"), ("cols", "disp"), None),
            P(),
            P(),
            P(),
        ),
        out_specs=P(("tiles", "rows"), ("cols", "disp")),
        check_vma=False,
    )
```

```python
import functools

import jax
import jax.numpy as jnp
from jax import lax
from jax.experimental import pallas as pl
from jax.experimental.pallas import tpu as pltpu
from jax.sharding import PartitionSpec as P

MID = 2
DDEV = 16


def extended_2(block, sides, width):
    for axis, dim in sides:
        count = lax.axis_size(axis)
        forward = [(i, i + 1) for i in range(count - 1)]
        backward = [(target, source) for source, target in forward]
        low = lax.ppermute(
            lax.slice_in_dim(block, block.shape[dim] - width, None, axis=dim), axis, forward
        )
        high = lax.ppermute(lax.slice_in_dim(block, 0, width, axis=dim), axis, backward)
        block = jnp.concatenate([low, block, high], axis=dim)
    return block


def passed_along(x, axis, by):
    peers = lax.axis_size(axis)
    pairs = [(i, i + by) for i in range(peers) if 0 <= i + by < peers]
    return lax.ppermute(x, axis, pairs)


def combined_all(part, axis, combine):
    gathered = jax.tree.map(lambda a: lax.all_gather(a, axis), part)

    def take(source):
        return jax.tree.map(lambda a: lax.dynamic_index_in_dim(a, source, 0, False), gathered)

    return lax.fori_loop(
        1, lax.axis_size(axis), lambda source, state: combine(state, take(source)), take(0)
    )


def correlate(left_full, extended, groups, first_disp, count, total_disp):
    rows_here, width_here, channels = left_full.shape
    group_size = channels // groups
    left_groups = left_full.reshape(rows_here, width_here, groups, group_size)

    def single(offset):
        disp_value = first_disp + offset
        shifted = lax.dynamic_slice_in_dim(extended, 2 * width_here - disp_value, width_here, 1)
        right_groups = shifted.reshape(rows_here, width_here, groups, group_size)
        corr = (
            jnp.einsum(
                "hwgc,hwgc->ghw", left_groups, right_groups, preferred_element_type=jnp.float32
            )
            / group_size
        )
        inside = (disp_value >= 0) & (disp_value < total_disp)
        return jnp.where(inside, corr, 0.0).astype(jnp.bfloat16)

    return lax.map(single, jnp.arange(count, dtype=jnp.int32))


def convolve(padded, kernel):
    depth_out = padded.shape[0] - 2
    in_chans = padded.shape[1]
    rows_out = padded.shape[2] - 2
    cols_out = padded.shape[3] - 2
    out_chans = kernel.shape[1]
    columns = jnp.concatenate(
        [
            padded[:, :, row_tap : row_tap + rows_out, col_tap : col_tap + cols_out]
            for row_tap in range(3)
            for col_tap in range(3)
        ],
        axis=1,
    )
    flat = columns.reshape(depth_out + 2, 9 * in_chans, rows_out * cols_out)
    summed = jnp.zeros((depth_out, out_chans, rows_out * cols_out), jnp.float32)
    for disp_tap in range(3):
        taps = (
            jnp.transpose(kernel[9 * disp_tap : 9 * disp_tap + 9], (1, 0, 2))
            .reshape(out_chans, 9 * in_chans)
            .astype(flat.dtype)
        )
        summed = summed + jnp.einsum(
            "ok,dkn->don",
            taps,
            flat[disp_tap : disp_tap + depth_out],
            preferred_element_type=jnp.float32,
            precision=lax.Precision.HIGHEST,
        )
    return summed.reshape(depth_out, out_chans, rows_out, cols_out)


def widen(hidden):
    return extended_2(hidden, (("disp", 0), ("rows", 2), ("cols", 3)), 1)


def combine_parts(earlier, later):
    highest = jnp.maximum(earlier[0], later[0])
    scale_one = jnp.exp(earlier[0] - highest)
    scale_two = jnp.exp(later[0] - highest)
    return (
        highest,
        earlier[1] * scale_one + later[1] * scale_two,
        earlier[2] * scale_one + later[2] * scale_two,
    )


def shards(left_feat, right_feat, conv_first, conv_mid, conv_last):
    piece_width = left_feat.shape[1]
    groups = conv_first.shape[2]
    disp_count = lax.axis_size("disp")
    depth_here = DDEV
    total_disp = depth_here * disp_count
    first_disp = lax.axis_index("disp") * depth_here
    left_full, right_full = (
        lax.all_gather(left_feat, "disp", axis=1, tiled=True),
        lax.all_gather(right_feat, "disp", axis=1, tiled=True),
    )
    prior_full = passed_along(right_full, "cols", 1)
    extended = jnp.concatenate([jnp.zeros_like(right_full), prior_full, right_full], axis=1)
    volume = correlate(left_full, extended, groups, first_disp, depth_here, total_disp)
    padded = extended_2(volume, (("disp", 0), ("rows", 2), ("cols", 3)), 1)
    hidden = jax.nn.relu(convolve(padded, conv_first))
    for layer in range(MID):
        hidden = jax.nn.relu(convolve(widen(hidden), conv_mid[layer]))
    cost_cube = convolve(widen(hidden), conv_last)[:, 0]
    levels = (
        (first_disp + jnp.arange(depth_here, dtype=jnp.int32)).astype(jnp.float32) / total_disp
    )[:, None, None]
    local_high = jnp.max(cost_cube, axis=0)
    weights = jnp.exp(cost_cube - local_high[None])
    merged = combined_all(
        (local_high, jnp.sum(weights, axis=0), jnp.sum(weights * levels, axis=0)),
        "disp",
        combine_parts,
    )
    whole_row = merged[2] / merged[1]
    return lax.dynamic_slice_in_dim(whole_row, lax.axis_index("disp") * piece_width, piece_width, 1)


HALO = 4
GROUP = 4
EDGE = 16
SLAB = 128


def build_permutation(perm_ref, channels, groups):
    size = channels // groups
    rows, lanes = perm_ref.shape
    part = rows // 2
    lane = lax.broadcasted_iota(jnp.int32, (1, lanes), 1)
    group = lane % 64
    for row in range(2):
        wanted = group * size + lane // SLAB
        wanted = jnp.where((group < groups) & ((lane // 64) % 2 == row), wanted, -1)
        channel = lax.broadcasted_iota(jnp.int32, (part, lanes), 0)
        block = (channel == wanted).astype(jnp.float32).astype(jnp.bfloat16)
        perm_ref[row * part : (row + 1) * part, :] = block


def tap_of(a, r_in, r_out, e):
    return 9 * a + 3 * (r_in - r_out + 1) + e


def place_first(target, at, lead, slabs):
    for a, slab in enumerate(slabs):
        lane = SLAB * (lead + a)
        target[at : at + slab.shape[0], lane : lane + SLAB] = slab


def build_first(taps_ref, pair_ref, quad_ref):
    pair_ref[...] = jnp.zeros_like(pair_ref)
    quad_ref[...] = jnp.zeros_like(quad_ref)
    outs, ins = taps_ref.shape[1:]
    blank = jnp.zeros((outs, 64 - ins), jnp.float32)
    for e in range(3):
        for r_out in range(2):
            slabs = []
            for a in range(3):
                parts = []
                for r_in in range(2):
                    parts += [taps_ref[tap_of(a, r_in, r_out, e)].astype(jnp.float32), blank]
                slabs.append(jnp.concatenate(parts, axis=1).astype(jnp.bfloat16))
            if e < 2:
                for d_out in range(2):
                    place_first(pair_ref, e * 128 + d_out * 64 + r_out * 32, d_out, slabs)
            else:
                for d_out in range(GROUP):
                    place_first(quad_ref, d_out * 64 + r_out * 32, d_out, slabs)


def place_mid(target, at, lead, block):
    for half in range(2):
        piece = block[:, SLAB * half : SLAB * half + SLAB]
        for copy in range(2):
            lane = 2 * SLAB * (lead + half) + SLAB * copy
            target[at : at + piece.shape[0], lane : lane + SLAB] = piece


def build_mid(taps_ref, pair_ref, quad_ref):
    pair_ref[...] = jnp.zeros_like(pair_ref)
    quad_ref[...] = jnp.zeros_like(quad_ref)
    outs = taps_ref.shape[1]
    blank = jnp.zeros((outs, 64), jnp.float32)
    for e in range(3):
        for r_out in range(2):
            slabs = [
                taps_ref[tap_of(a, r_in, r_out, e)].astype(jnp.float32)
                for a in range(3)
                for r_in in range(2)
            ]
            shifted = (
                jnp.concatenate(slabs + [blank], axis=1).astype(jnp.bfloat16),
                jnp.concatenate([blank] + slabs, axis=1).astype(jnp.bfloat16),
            )
            if e < 2:
                for d_out in range(2):
                    place_mid(pair_ref, e * 128 + d_out * 64 + r_out * 32, 0, shifted[d_out])
            else:
                for d_out in range(GROUP):
                    place_mid(
                        quad_ref, d_out * 64 + r_out * 32, d_out // 2, shifted[d_out % 2]
                    )


def build_last(taps_ref, line_ref, row):
    taps = taps_ref[...].astype(jnp.float32)
    lines = []
    for e in range(3):
        for d_out in range(GROUP):
            parts = []
            for a in range(3):
                for r_in in range(2):
                    upper, lower = (tap_of(a, r_in, r_out, e) for r_out in range(2))
                    parts.append(
                        jnp.where(row == 0, taps[upper : upper + 1], taps[lower : lower + 1])
                    )
            if d_out > 0:
                parts.insert(0, jnp.zeros((1, 64 * d_out), jnp.float32))
            if d_out < GROUP - 1:
                parts.append(jnp.zeros((1, 64 * (GROUP - 1 - d_out)), jnp.float32))
            lines.append(jnp.concatenate(parts, axis=1))
        lines.append(jnp.zeros((8 - GROUP, 3 * SLAB), jnp.float32))
    lines.append(jnp.zeros((8, 3 * SLAB), jnp.float32))
    block = jnp.concatenate(lines, axis=0).astype(jnp.bfloat16)
    for pair in range(3):
        piece = block[:, SLAB * pair : SLAB * pair + SLAB]
        for copy in range(2):
            lane = SLAB * (2 * pair + copy)
            line_ref[:, lane : lane + SLAB] = piece


def across(x, banded):
    return lax.dot_general(
        x, banded, (((1,), (1,)), ((), ())), preferred_element_type=jnp.float32
    )


def exchange_plan(width):
    own = EDGE + 2 * width
    left_at = own + width + EDGE
    near = []
    for other in (1, 0):
        near.append((1, -1, other, 0, own + width, EDGE))
        near.append((0, -1, other, 0, left_at + EDGE + width, EDGE))
    near.append((1, 0, 1, 0, own, width))
    near.append((0, 0, 1, 0, left_at + EDGE, width))
    for other in (1, 0):
        near.append((1, 1, other, 0, own - width, width))
        near.append((0, 1, other, width - EDGE, left_at, EDGE))
    far = [(1, 2, other, 0, own - 2 * width, width) for other in (1, 0)]
    far += [(1, 3, other, width - EDGE, 0, EDGE) for other in (1, 0)]
    return tuple(near), tuple(far), own, left_at, left_at + width + 2 * EDGE


def exchange_steps(left_ref, right_ref, held, send_sem, recv_sem, own_sem, told_sem):
    width, channels = left_ref.shape[1:]
    near, far, own, left_at, _ = exchange_plan(width)
    copies = near + far
    row, col, disp = lax.axis_index("rows"), lax.axis_index("cols"), lax.axis_index("disp")
    col_disps = lax.axis_size("disp")
    pieces = col_disps * lax.axis_size("cols")
    piece = col * col_disps + disp
    barrier = pltpu.get_barrier_semaphore()
    partners = sorted({(by, other) for _, by, other, _, _, _ in near})
    distant = sorted({(by, other) for _, by, other, _, _, _ in far})

    def device(other, by):
        target = piece + by
        target_col = (target >= col_disps).astype(jnp.int32)
        return {
            "tiles": lax.axis_index("tiles"),
            "disp": target - col_disps * target_col,
            "rows": 1 - row if other else row,
            "cols": target_col,
        }

    def exists(by):
        return (piece + by >= 0) & (piece + by < pieces)

    def crosses(by):
        return exists(by) & ((disp + by < 0) | (disp + by >= col_disps))

    def stays(by):
        return (disp + by >= 0) & (disp + by < col_disps)

    def landing(target, count):
        return held.at[row, pl.ds(target, count)]

    def copy(number):
        view, by, other, source, target, count = copies[number]
        return pltpu.make_async_remote_copy(
            src_ref=landing((own if view else left_at + EDGE) + source, count),
            dst_ref=landing(target, count),
            send_sem=send_sem.at[number],
            recv_sem=recv_sem.at[number],
            device_id=device(other, by),
            device_id_type=pl.DeviceIdType.MESH,
        )

    own_loads = [
        pltpu.make_async_copy(source.at[0], landing(target, width), own_sem.at[number])
        for number, (source, target) in enumerate(
            ((left_ref, left_at + EDGE), (right_ref, own))
        )
    ]

    def tell(semaphore, by, other):
        pl.semaphore_signal(
            semaphore, inc=1, device_id=device(other, by), device_id_type=pl.DeviceIdType.MESH
        )

    def greet():
        held[...] = jnp.zeros_like(held)
        for by, other in partners:

            @pl.when(exists(by))
            def _():
                tell(barrier, by, other)

        for by, other in distant:

            @pl.when(crosses(-by))
            def _():
                tell(barrier, -by, other)

        for load in own_loads:
            load.start()

    def start(numbers, among):
        for number in numbers:

            @pl.when(among(copies[number][1]))
            def _():
                copy(number).start()

    def send_near():
        count = jnp.int32(0)
        for by, _ in partners:
            count = count + exists(by).astype(jnp.int32)
        for by, _ in distant:
            count = count + crosses(by).astype(jnp.int32)
        pl.semaphore_wait(barrier, count)
        for load in own_loads:
            load.wait()

        @pl.when(stays(-1) & stays(1))
        def _():
            tell(told_sem.at[0], -1, 0)

        start(range(6, 10), crosses)
        start(range(4, 6), exists)
        start(range(10, 14), crosses)
        start(range(6, 10), stays)
        start(range(4), exists)

    def send_far(step):
        @pl.when(stays(step + 2))
        def _():
            pl.semaphore_wait(told_sem.at[step], 1)

        if step == 0:

            @pl.when(stays(-1) & stays(2))
            def _():
                tell(told_sem.at[1], -1, 0)

        start(range(len(near) + 2 * step, len(near) + 2 * step + 2), stays)

    def receive(numbers):
        for number in numbers:

            @pl.when(exists(-copies[number][1]))
            def _():
                copy(number).wait_recv()

    def receive_near():
        receive(range(len(near)))

    def receive_far():
        receive(range(len(near), len(copies)))

    def finish():
        for number in range(len(copies)):

            @pl.when(exists(copies[number][1]))
            def _():
                copy(number).wait_send()

    return greet, send_near, send_far, receive_near, receive_far, finish


def whole_kernel(
    disps,
    width_all,
    left_ref,
    right_ref,
    first_hbm,
    mid_hbm,
    last_hbm,
    out_ref,
    feat_ref,
    send_sem,
    recv_sem,
    own_sem,
    told_sem,
    load_sem,
    perm_ref,
    first_taps,
    mid_taps,
    last_taps,
    a_ref,
    p_ref,
    f_ref,
    pair_ref,
    quad_ref,
    line_ref,
):
    width_here = out_ref.shape[1]
    wide = width_here + 2 * HALO
    groups_d = disps // GROUP + 1
    channels, groups = left_ref.shape[2], first_taps.shape[2]
    size = channels // groups
    _, _, own, left_at, held_rows = exchange_plan(width_here)
    greet, send_near, send_far, receive_near, receive_far, finish = exchange_steps(
        left_ref, right_ref, feat_ref, send_sem, recv_sem, own_sem, told_sem
    )
    loads = [
        pltpu.make_async_copy(source, target, load_sem.at[number])
        for number, (source, target) in enumerate(
            ((first_hbm, first_taps), (mid_hbm, mid_taps), (last_hbm, last_taps))
        )
    ]
    greet()
    for load in loads:
        load.start()
    send_near()
    build_permutation(perm_ref, channels, groups)
    a_ref[0, 0:wide, :] = jnp.zeros((wide, 6 * SLAB), jnp.bfloat16)
    for layer in range(MID + 2):
        a_ref[layer, (groups_d - 1) * wide : groups_d * wide, 4 * SLAB :] = jnp.zeros(
            (wide, 2 * SLAB), jnp.bfloat16
        )
    loads[0].wait()
    build_first(first_taps, pair_ref.at[0], quad_ref.at[0])
    send_far(0)
    loads[1].wait()
    for layer in range(MID):
        build_mid(mid_taps.at[layer], pair_ref.at[layer + 1], quad_ref.at[layer + 1])
    send_far(1)
    loads[2].wait()
    build_last(last_taps, line_ref, lax.axis_index("rows"))

    def permute(start, stop):
        for at in range(0, size * SLAB, 2 * SLAB):
            lanes = slice(at, at + 2 * SLAB)
            both = jnp.dot(
                feat_ref[0, start:stop],
                perm_ref[0:channels, lanes],
                preferred_element_type=jnp.float32,
            ) + jnp.dot(
                feat_ref[1, start:stop],
                perm_ref[channels : 2 * channels, lanes],
                preferred_element_type=jnp.float32,
            )
            f_ref[at // SLAB, start:stop] = both[:, :SLAB]
            f_ref[at // SLAB + 1, start:stop] = both[:, SLAB:]

    def volume(start, stop):
        for group in range(start, stop):
            sums = [None] * GROUP
            for k in range(size):
                left = f_ref[k, left_at + EDGE - HALO : left_at + EDGE - HALO + wide]
                for place in range(GROUP):
                    at = own - HALO - (GROUP * (group - 1) + place)
                    term = left * f_ref[k, at : at + wide]
                    sums[place] = term if k == 0 else sums[place] + term
            for place in range(GROUP):
                slab = (sums[place] / size).astype(jnp.bfloat16)
                here = slice(group * wide, (group + 1) * wide)
                a_ref[0, here, SLAB * place : SLAB * place + SLAB] = slab
                if place < 2:
                    before = slice((group - 1) * wide, group * wide)
                    lane = SLAB * (GROUP + place)
                    a_ref[0, before, lane : lane + SLAB] = slab

    piece = lax.axis_index("cols") * lax.axis_size("disp") + lax.axis_index("disp")
    column = piece * width_here - HALO + lax.broadcasted_iota(jnp.int32, (wide, SLAB), 0)
    in_image = (column >= 0) & (column < width_all)
    lane_disp = lax.broadcasted_iota(jnp.int32, (wide, SLAB), 1) // 64

    def products(layer, start, stop):
        source, part = a_ref.at[layer], p_ref.at[layer]
        middle = (start + stop) // 2

        def multiply(slab, first, last, lanes, taps_ref):
            rows = slice(first * wide, last * wide)
            got = across(source[rows, lanes], taps_ref[layer])
            held = slice(8 + first * wide, 8 + last * wide)
            part[slab, held] = got[:, :SLAB]
            part[slab + 1, held] = got[:, SLAB:]

        multiply(0, start, stop, slice(0, 4 * SLAB), pair_ref)
        multiply(2, start, stop, slice(2 * SLAB, 6 * SLAB), pair_ref)
        multiply(4, start, middle, slice(0, 6 * SLAB), quad_ref)
        multiply(4, middle, stop, slice(0, 6 * SLAB), quad_ref)

    def finish_layer(layer, start, stop):
        target, part = a_ref.at[layer + 1], p_ref.at[layer]
        base = layer + 1 - HALO
        for group in range(start, stop):
            at = 8 + group * wide
            here = slice(group * wide, (group + 1) * wide)
            before = slice((group - 1) * wide, group * wide)
            for half in range(2):
                total = (
                    part[2 * half, at - 1 : at - 1 + wide]
                    + part[2 * half + 1, at : at + wide]
                    + part[4 + half, at + 1 : at + 1 + wide]
                )
                low = base + GROUP * group + 2 * half
                keep = in_image
                if low < 0 or low + 2 > disps:
                    keep = keep & (lane_disp >= -low) & (lane_disp < disps - low)
                total = jnp.where(keep, jnp.maximum(total, 0.0), 0.0)
                high = total.astype(jnp.bfloat16)
                rest = (total - high.astype(jnp.float32)).astype(jnp.bfloat16)
                lane = 2 * SLAB * half
                target[here, lane : lane + SLAB] = high
                target[here, lane + SLAB : lane + 2 * SLAB] = rest
                if half == 0 and group > 0:
                    target[before, 4 * SLAB : 5 * SLAB] = high
                    target[before, 5 * SLAB : 6 * SLAB] = rest

    receive_near()
    receive_far()
    permute(0, held_rows)
    volume(1, groups_d)
    for layer in range(MID + 1):
        products(layer, 0, groups_d)
        finish_layer(layer, 0, groups_d)

    per = SLAB // wide
    lane = lax.broadcasted_iota(jnp.int32, (8, SLAB), 1)
    place = lax.broadcasted_iota(jnp.int32, (8, SLAB), 0)
    within = lane // wide
    costs = []
    valids = []
    for first in range(0, groups_d - 1, per):
        taken = a_ref[MID + 1, first * wide : first * wide + SLAB]
        parts = across(line_ref[...], taken)
        cost = (
            pltpu.roll(parts[0:8], 1, 1) + parts[8:16] + pltpu.roll(parts[16:24], SLAB - 1, 1)
        )
        valid = (place < GROUP) & (within < min(per, groups_d - 1 - first))
        valids.append(valid)
        costs.append(jnp.where(valid, cost, -jnp.inf))
    def gathered(x, combine):
        return functools.reduce(
            combine, [x] + [pltpu.roll(x, SLAB - wide * k, 1) for k in range(1, per)]
        )

    top = jnp.max(functools.reduce(jnp.maximum, costs), axis=0, keepdims=True)
    top = gathered(jnp.broadcast_to(top, (8, SLAB)), jnp.maximum)
    tops = top
    for k in range(1, per):
        tops = jnp.where(within == k, pltpu.roll(top, wide * k, 1), tops)
    weight_sum = jnp.zeros((8, SLAB), jnp.float32)
    level_sum = jnp.zeros((8, SLAB), jnp.float32)
    for number, cost in enumerate(costs):
        weight = jnp.where(valids[number], jnp.exp(cost - tops), 0.0)
        level = GROUP * (number * per + within) + place
        weight_sum += weight
        level_sum += weight * (level.astype(jnp.float32) * (1.0 / disps))
    weight_sum = gathered(jnp.broadcast_to(jnp.sum(weight_sum, axis=0, keepdims=True), (8, SLAB)), jnp.add)
    level_sum = gathered(jnp.broadcast_to(jnp.sum(level_sum, axis=0, keepdims=True), (8, SLAB)), jnp.add)
    line = pltpu.roll(level_sum / weight_sum, SLAB - HALO, 1)
    out_ref[...] = line[0:1, 0:width_here]
    finish()


def window_shards(left_feat, right_feat, conv_first, conv_mid, conv_last):
    width = left_feat.shape[1]
    channels = left_feat.shape[2]
    groups = conv_first.shape[2]
    disps = DDEV * lax.axis_size("disp")
    width_all = width * lax.axis_size("disp") * lax.axis_size("cols")
    near, far, _, _, held_rows = exchange_plan(width)
    count = len(near) + len(far)
    wide = width + 2 * HALO
    rows = (disps // GROUP + 1) * wide
    size = channels // groups
    return pl.pallas_call(
        functools.partial(whole_kernel, disps, width_all),
        out_shape=pltpu.VMEM((1, width), jnp.float32),
        in_specs=[pl.BlockSpec(memory_space=pltpu.HBM)] * 5,
        out_specs=pl.BlockSpec(memory_space=pltpu.VMEM),
        scratch_shapes=[
            pltpu.VMEM((2, held_rows, channels), jnp.bfloat16),
            pltpu.SemaphoreType.DMA((count,)),
            pltpu.SemaphoreType.DMA((count,)),
            pltpu.SemaphoreType.DMA((2,)),
            pltpu.SemaphoreType.REGULAR((2,)),
            pltpu.SemaphoreType.DMA((3,)),
            pltpu.VMEM((2 * channels, size * SLAB), jnp.bfloat16),
            pltpu.VMEM(conv_first.shape, jnp.bfloat16),
            pltpu.VMEM(conv_mid.shape, jnp.bfloat16),
            pltpu.VMEM((27, conv_last.shape[2]), jnp.bfloat16),
            pltpu.VMEM((MID + 2, rows + 2 * wide, 6 * SLAB), jnp.bfloat16),
            pltpu.VMEM((MID + 1, 6, rows + 16, SLAB), jnp.float32),
            pltpu.VMEM((size, held_rows, SLAB), jnp.float32),
            pltpu.VMEM((MID + 1, 2 * SLAB, 4 * SLAB), jnp.bfloat16),
            pltpu.VMEM((MID + 1, 2 * SLAB, 6 * SLAB), jnp.bfloat16),
            pltpu.VMEM((32, 6 * SLAB), jnp.bfloat16),
        ],
        compiler_params=pltpu.CompilerParams(
            vmem_limit_bytes=56 * 1024 * 1024, collective_id=0, has_side_effects=True
        ),
    )(left_feat, right_feat, conv_first, conv_mid, conv_last.reshape(27, -1))


def solution(mesh):
    rows, pieces = mesh.shape["rows"], mesh.shape["cols"] * mesh.shape["disp"]
    body = window_shards if rows == 2 and mesh.shape["disp"] == 4 and pieces == 8 else shards
    return jax.shard_map(
        body,
        mesh=mesh,
        in_specs=(
            P(("tiles", "rows"), ("cols", "disp"), None),
            P(("tiles", "rows"), ("cols", "disp"), None),
            P(),
            P(),
            P(),
        ),
        out_specs=P(("tiles", "rows"), ("cols", "disp")),
        check_vma=False,
    )
```

```python
import functools

import jax
import jax.numpy as jnp
from jax import lax
from jax.experimental import pallas as pl
from jax.experimental.pallas import tpu as pltpu
from jax.sharding import PartitionSpec as P

MID = 2
DDEV = 16


def extended_2(block, sides, width):
    for axis, dim in sides:
        count = lax.axis_size(axis)
        forward = [(i, i + 1) for i in range(count - 1)]
        backward = [(target, source) for source, target in forward]
        low = lax.ppermute(
            lax.slice_in_dim(block, block.shape[dim] - width, None, axis=dim), axis, forward
        )
        high = lax.ppermute(lax.slice_in_dim(block, 0, width, axis=dim), axis, backward)
        block = jnp.concatenate([low, block, high], axis=dim)
    return block


def passed_along(x, axis, by):
    peers = lax.axis_size(axis)
    pairs = [(i, i + by) for i in range(peers) if 0 <= i + by < peers]
    return lax.ppermute(x, axis, pairs)


def combined_all(part, axis, combine):
    gathered = jax.tree.map(lambda a: lax.all_gather(a, axis), part)

    def take(source):
        return jax.tree.map(lambda a: lax.dynamic_index_in_dim(a, source, 0, False), gathered)

    return lax.fori_loop(
        1, lax.axis_size(axis), lambda source, state: combine(state, take(source)), take(0)
    )


def correlate(left_full, extended, groups, first_disp, count, total_disp):
    rows_here, width_here, channels = left_full.shape
    group_size = channels // groups
    left_groups = left_full.reshape(rows_here, width_here, groups, group_size)

    def single(offset):
        disp_value = first_disp + offset
        shifted = lax.dynamic_slice_in_dim(extended, 2 * width_here - disp_value, width_here, 1)
        right_groups = shifted.reshape(rows_here, width_here, groups, group_size)
        corr = (
            jnp.einsum(
                "hwgc,hwgc->ghw", left_groups, right_groups, preferred_element_type=jnp.float32
            )
            / group_size
        )
        inside = (disp_value >= 0) & (disp_value < total_disp)
        return jnp.where(inside, corr, 0.0).astype(jnp.bfloat16)

    return lax.map(single, jnp.arange(count, dtype=jnp.int32))


def convolve(padded, kernel):
    depth_out = padded.shape[0] - 2
    in_chans = padded.shape[1]
    rows_out = padded.shape[2] - 2
    cols_out = padded.shape[3] - 2
    out_chans = kernel.shape[1]
    columns = jnp.concatenate(
        [
            padded[:, :, row_tap : row_tap + rows_out, col_tap : col_tap + cols_out]
            for row_tap in range(3)
            for col_tap in range(3)
        ],
        axis=1,
    )
    flat = columns.reshape(depth_out + 2, 9 * in_chans, rows_out * cols_out)
    summed = jnp.zeros((depth_out, out_chans, rows_out * cols_out), jnp.float32)
    for disp_tap in range(3):
        taps = (
            jnp.transpose(kernel[9 * disp_tap : 9 * disp_tap + 9], (1, 0, 2))
            .reshape(out_chans, 9 * in_chans)
            .astype(flat.dtype)
        )
        summed = summed + jnp.einsum(
            "ok,dkn->don",
            taps,
            flat[disp_tap : disp_tap + depth_out],
            preferred_element_type=jnp.float32,
            precision=lax.Precision.HIGHEST,
        )
    return summed.reshape(depth_out, out_chans, rows_out, cols_out)


def widen(hidden):
    return extended_2(hidden, (("disp", 0), ("rows", 2), ("cols", 3)), 1)


def combine_parts(earlier, later):
    highest = jnp.maximum(earlier[0], later[0])
    scale_one = jnp.exp(earlier[0] - highest)
    scale_two = jnp.exp(later[0] - highest)
    return (
        highest,
        earlier[1] * scale_one + later[1] * scale_two,
        earlier[2] * scale_one + later[2] * scale_two,
    )


def shards(left_feat, right_feat, conv_first, conv_mid, conv_last):
    piece_width = left_feat.shape[1]
    groups = conv_first.shape[2]
    disp_count = lax.axis_size("disp")
    depth_here = DDEV
    total_disp = depth_here * disp_count
    first_disp = lax.axis_index("disp") * depth_here
    left_full, right_full = (
        lax.all_gather(left_feat, "disp", axis=1, tiled=True),
        lax.all_gather(right_feat, "disp", axis=1, tiled=True),
    )
    prior_full = passed_along(right_full, "cols", 1)
    extended = jnp.concatenate([jnp.zeros_like(right_full), prior_full, right_full], axis=1)
    volume = correlate(left_full, extended, groups, first_disp, depth_here, total_disp)
    padded = extended_2(volume, (("disp", 0), ("rows", 2), ("cols", 3)), 1)
    hidden = jax.nn.relu(convolve(padded, conv_first))
    for layer in range(MID):
        hidden = jax.nn.relu(convolve(widen(hidden), conv_mid[layer]))
    cost_cube = convolve(widen(hidden), conv_last)[:, 0]
    levels = (
        (first_disp + jnp.arange(depth_here, dtype=jnp.int32)).astype(jnp.float32) / total_disp
    )[:, None, None]
    local_high = jnp.max(cost_cube, axis=0)
    weights = jnp.exp(cost_cube - local_high[None])
    merged = combined_all(
        (local_high, jnp.sum(weights, axis=0), jnp.sum(weights * levels, axis=0)),
        "disp",
        combine_parts,
    )
    whole_row = merged[2] / merged[1]
    return lax.dynamic_slice_in_dim(whole_row, lax.axis_index("disp") * piece_width, piece_width, 1)


HALO = 4
GROUP = 4
EDGE = 8
BLOCK = 8
SLAB = 128


def build_permutation(perm_ref, channels, groups):
    size = channels // groups
    rows, lanes = perm_ref.shape
    part = rows // 2
    lane = lax.broadcasted_iota(jnp.int32, (1, lanes), 1)
    group = lane % 64
    for row in range(2):
        wanted = group * size + lane // SLAB
        wanted = jnp.where((group < groups) & ((lane // 64) % 2 == row), wanted, -1)
        channel = lax.broadcasted_iota(jnp.int32, (part, lanes), 0)
        block = (channel == wanted).astype(jnp.float32).astype(jnp.bfloat16)
        perm_ref[row * part : (row + 1) * part, :] = block


def tap_of(a, r_in, r_out, e):
    return 9 * a + 3 * (r_in - r_out + 1) + e


def place_first(target, at, lead, slabs):
    for a, slab in enumerate(slabs):
        lane = SLAB * (lead + a)
        target[at : at + slab.shape[0], lane : lane + SLAB] = slab


def build_first(taps_ref, pair_ref, quad_ref):
    pair_ref[...] = jnp.zeros_like(pair_ref)
    quad_ref[...] = jnp.zeros_like(quad_ref)
    outs, ins = taps_ref.shape[1:]
    blank = jnp.zeros((outs, 64 - ins), jnp.float32)
    for e in range(3):
        for r_out in range(2):
            slabs = []
            for a in range(3):
                parts = []
                for r_in in range(2):
                    parts += [taps_ref[tap_of(a, r_in, r_out, e)].astype(jnp.float32), blank]
                slabs.append(jnp.concatenate(parts, axis=1).astype(jnp.bfloat16))
            if e < 2:
                for d_out in range(2):
                    place_first(pair_ref, e * 128 + d_out * 64 + r_out * 32, d_out, slabs)
            else:
                for d_out in range(GROUP):
                    place_first(quad_ref, d_out * 64 + r_out * 32, d_out, slabs)


def place_mid(target, at, lead, block):
    for half in range(2):
        piece = block[:, SLAB * half : SLAB * half + SLAB]
        for copy in range(2):
            lane = 2 * SLAB * (lead + half) + SLAB * copy
            target[at : at + piece.shape[0], lane : lane + SLAB] = piece


def build_mid(taps_ref, pair_ref, quad_ref):
    pair_ref[...] = jnp.zeros_like(pair_ref)
    quad_ref[...] = jnp.zeros_like(quad_ref)
    outs = taps_ref.shape[1]
    blank = jnp.zeros((outs, 64), jnp.float32)
    for e in range(3):
        for r_out in range(2):
            slabs = [
                taps_ref[tap_of(a, r_in, r_out, e)].astype(jnp.float32)
                for a in range(3)
                for r_in in range(2)
            ]
            shifted = (
                jnp.concatenate(slabs + [blank], axis=1).astype(jnp.bfloat16),
                jnp.concatenate([blank] + slabs, axis=1).astype(jnp.bfloat16),
            )
            if e < 2:
                for d_out in range(2):
                    place_mid(pair_ref, e * 128 + d_out * 64 + r_out * 32, 0, shifted[d_out])
            else:
                for d_out in range(GROUP):
                    place_mid(
                        quad_ref, d_out * 64 + r_out * 32, d_out // 2, shifted[d_out % 2]
                    )


def build_last(taps_ref, line_ref, row):
    taps = taps_ref[...].astype(jnp.float32)
    lines = []
    for e in range(3):
        for d_out in range(GROUP):
            parts = []
            for a in range(3):
                for r_in in range(2):
                    upper, lower = (tap_of(a, r_in, r_out, e) for r_out in range(2))
                    parts.append(
                        jnp.where(row == 0, taps[upper : upper + 1], taps[lower : lower + 1])
                    )
            if d_out > 0:
                parts.insert(0, jnp.zeros((1, 64 * d_out), jnp.float32))
            if d_out < GROUP - 1:
                parts.append(jnp.zeros((1, 64 * (GROUP - 1 - d_out)), jnp.float32))
            lines.append(jnp.concatenate(parts, axis=1))
        lines.append(jnp.zeros((8 - GROUP, 3 * SLAB), jnp.float32))
    lines.append(jnp.zeros((8, 3 * SLAB), jnp.float32))
    block = jnp.concatenate(lines, axis=0).astype(jnp.bfloat16)
    for pair in range(3):
        piece = block[:, SLAB * pair : SLAB * pair + SLAB]
        for copy in range(2):
            lane = SLAB * (2 * pair + copy)
            line_ref[:, lane : lane + SLAB] = piece


def across(x, banded):
    return lax.dot_general(
        x, banded, (((1,), (1,)), ((), ())), preferred_element_type=jnp.float32
    )


def exchange_plan(width):
    own = EDGE + 2 * width
    left_at = own + width + EDGE
    near = []
    for other in (1, 0):
        near.append((1, -1, other, 0, own + width, EDGE))
        near.append((0, -1, other, 0, left_at + EDGE + width, EDGE))
    near.append((1, 0, 1, 0, own, width))
    near.append((0, 0, 1, 0, left_at + EDGE, width))
    for other in (1, 0):
        near.append((1, 1, other, 0, own - width, width))
        near.append((0, 1, other, width - EDGE, left_at, EDGE))
    far = [(1, 2, other, 0, own - 2 * width, width) for other in (1, 0)]
    far += [(1, 3, other, width - EDGE, 0, EDGE) for other in (1, 0)]
    return tuple(near), tuple(far), own, left_at, left_at + width + 2 * EDGE


def exchange_steps(left_ref, right_ref, held, send_sem, recv_sem, own_sem, told_sem):
    width = left_ref.shape[0] * BLOCK
    near, far, own, left_at, _ = exchange_plan(width)
    copies = near + far
    row, col, disp = lax.axis_index("rows"), lax.axis_index("cols"), lax.axis_index("disp")
    col_disps = lax.axis_size("disp")
    pieces = col_disps * lax.axis_size("cols")
    piece = col * col_disps + disp
    barrier = pltpu.get_barrier_semaphore()
    reach = max(abs(by) for _, by, _, _, _, _ in copies)
    steps = sorted({by for _, by, _, _, _, _ in copies if by})
    related = [by for by in range(-reach, reach + 1) if by]

    def device(other, by):
        target = piece + by
        target_col = (target >= col_disps).astype(jnp.int32)
        return {
            "tiles": lax.axis_index("tiles"),
            "disp": target - col_disps * target_col,
            "rows": 1 - row if other else row,
            "cols": target_col,
        }

    def exists(by):
        return (piece + by >= 0) & (piece + by < pieces)

    def stays(by):
        return (disp + by >= 0) & (disp + by < col_disps)

    def lower(by):
        return stays(by) if by < 0 else exists(by) & (disp + by >= col_disps)

    def higher(by):
        return stays(by) if by > 0 else exists(by) & (disp + by < 0)

    def landing(target, count):
        return held.at[row, pl.ds(target // BLOCK, count // BLOCK)]

    def copy(number):
        view, by, other, source, target, count = copies[number]
        return pltpu.make_async_remote_copy(
            src_ref=landing((own if view else left_at + EDGE) + source, count),
            dst_ref=landing(target, count),
            send_sem=send_sem.at[number],
            recv_sem=recv_sem.at[number],
            device_id=device(other, by),
            device_id_type=pl.DeviceIdType.MESH,
        )

    own_loads = [
        pltpu.make_async_copy(source, landing(target, width), own_sem.at[number])
        for number, (source, target) in enumerate(
            ((left_ref, left_at + EDGE), (right_ref, own))
        )
    ]

    def tell(semaphore, by, other):
        pl.semaphore_signal(
            semaphore, inc=1, device_id=device(other, by), device_id_type=pl.DeviceIdType.MESH
        )

    def greet():
        held[...] = jnp.zeros_like(held)
        tell(barrier, 0, 1)
        for by in related:

            @pl.when(higher(by))
            def _():
                for other in range(2):
                    tell(barrier, by, other)

        for load in own_loads:
            load.start()

    def start(by):
        for number, (_, step, _, _, _, _) in enumerate(copies):
            if step == by:
                copy(number).start()

    def meet():
        count = jnp.int32(1)
        for by in related:
            count = count + 2 * lower(by).astype(jnp.int32)
        pl.semaphore_wait(barrier, count)
        for by in steps:

            @pl.when(lower(-by))
            def _():
                for other in range(2):
                    tell(told_sem.at[steps.index(by)], -by, other)

        for load in own_loads:
            load.wait()

    def send(by):
        if by == 0:
            start(by)
        else:

            @pl.when(lower(by))
            def _():
                start(by)

    def send_told(by):
        @pl.when(higher(by))
        def _():
            pl.semaphore_wait(told_sem.at[steps.index(by)], 2)
            start(by)

    def receive(numbers):
        for number in numbers:

            @pl.when(exists(-copies[number][1]))
            def _():
                copy(number).wait_recv()

    def receive_near():
        receive(range(len(near)))

    def receive_far():
        receive(range(len(near), len(copies)))

    def finish():
        for number in range(len(copies)):

            @pl.when(exists(copies[number][1]))
            def _():
                copy(number).wait_send()

    return greet, meet, send, send_told, receive_near, receive_far, finish


def whole_kernel(
    disps,
    width_all,
    left_ref,
    right_ref,
    first_hbm,
    mid_hbm,
    last_hbm,
    out_ref,
    feat_ref,
    send_sem,
    recv_sem,
    own_sem,
    told_sem,
    load_sem,
    perm_ref,
    first_taps,
    mid_taps,
    last_taps,
    a_ref,
    p_ref,
    f_ref,
    pair_ref,
    quad_ref,
    line_ref,
    kpair_ref,
    kquad_ref,
):
    width_here = out_ref.shape[1]
    wide = width_here + 2 * HALO
    groups_d = disps // GROUP + 1
    channels, groups = left_ref.shape[2], first_taps.shape[2]
    size = channels // groups
    _, _, own, left_at, held_rows = exchange_plan(width_here)
    greet, meet, send, send_told, receive_near, receive_far, finish = exchange_steps(
        left_ref, right_ref, feat_ref, send_sem, recv_sem, own_sem, told_sem
    )
    loads = [
        pltpu.make_async_copy(source, target, load_sem.at[number])
        for number, (source, target) in enumerate(
            ((first_hbm, first_taps), (mid_hbm, mid_taps), (last_hbm, last_taps))
        )
    ]
    greet()
    for load in loads:
        load.start()
    meet()
    for by in (1, 0, 2, 3, -1):
        send(by)
    build_permutation(perm_ref, channels, groups)
    send_told(1)
    a_ref[0, 0:wide, :] = jnp.zeros((wide, 6 * SLAB), jnp.bfloat16)
    for layer in range(MID + 2):
        a_ref[layer, (groups_d - 1) * wide : groups_d * wide, 4 * SLAB :] = jnp.zeros(
            (wide, 2 * SLAB), jnp.bfloat16
        )
    loads[0].wait()
    build_first(first_taps, pair_ref.at[0], quad_ref.at[0])
    send_told(2)
    loads[1].wait()
    for layer in range(MID):
        build_mid(mid_taps.at[layer], pair_ref.at[layer + 1], quad_ref.at[layer + 1])
    loads[2].wait()
    for layer in range(MID + 1):
        kpair_ref[layer] = pair_ref[layer].T
        kquad_ref[layer] = quad_ref[layer].T
    build_last(last_taps, line_ref, lax.axis_index("rows"))

    def permute(start, stop):
        held = [
            feat_ref[row, start // BLOCK : stop // BLOCK].reshape(stop - start, channels)
            for row in range(2)
        ]
        for at in range(0, size * SLAB, 2 * SLAB):
            lanes = slice(at, at + 2 * SLAB)
            both = jnp.dot(
                held[0],
                perm_ref[0:channels, lanes],
                preferred_element_type=jnp.float32,
            ) + jnp.dot(
                held[1],
                perm_ref[channels : 2 * channels, lanes],
                preferred_element_type=jnp.float32,
            )
            f_ref[at // SLAB, start:stop] = both[:, :SLAB]
            f_ref[at // SLAB + 1, start:stop] = both[:, SLAB:]

    def volume(start, stop):
        for group in range(start, stop):
            sums = [None] * GROUP
            for k in range(size):
                left = f_ref[k, left_at + EDGE - HALO : left_at + EDGE - HALO + wide]
                for place in range(GROUP):
                    at = own - HALO - (GROUP * (group - 1) + place)
                    term = left * f_ref[k, at : at + wide]
                    sums[place] = term if k == 0 else sums[place] + term
            for place in range(GROUP):
                slab = (sums[place] / size).astype(jnp.bfloat16)
                here = slice(group * wide, (group + 1) * wide)
                a_ref[0, here, SLAB * place : SLAB * place + SLAB] = slab
                if place < 2:
                    before = slice((group - 1) * wide, group * wide)
                    lane = SLAB * (GROUP + place)
                    a_ref[0, before, lane : lane + SLAB] = slab

    piece = lax.axis_index("cols") * lax.axis_size("disp") + lax.axis_index("disp")
    column = piece * width_here - HALO + lax.broadcasted_iota(jnp.int32, (wide, SLAB), 0)
    in_image = (column >= 0) & (column < width_all)
    lane_disp = lax.broadcasted_iota(jnp.int32, (wide, SLAB), 1) // 64

    def products(layer, start, stop):
        source, part = a_ref.at[layer], p_ref.at[layer]
        middle = (start + stop) // 2

        def multiply(slab, first, last, lanes, taps_ref):
            rows = slice(first * wide, last * wide)
            got = jnp.dot(source[rows, lanes], taps_ref[layer], preferred_element_type=jnp.float32)
            held = slice(8 + first * wide, 8 + last * wide)
            part[slab, held] = got[:, :SLAB]
            part[slab + 1, held] = got[:, SLAB:]

        multiply(0, start, stop, slice(0, 4 * SLAB), kpair_ref)
        multiply(2, start, stop, slice(2 * SLAB, 6 * SLAB), kpair_ref)
        multiply(4, start, middle, slice(0, 6 * SLAB), kquad_ref)
        multiply(4, middle, stop, slice(0, 6 * SLAB), kquad_ref)

    def finish_layer(layer, start, stop):
        target, part = a_ref.at[layer + 1], p_ref.at[layer]
        base = layer + 1 - HALO
        for group in range(start, stop):
            at = 8 + group * wide
            here = slice(group * wide, (group + 1) * wide)
            before = slice((group - 1) * wide, group * wide)
            for half in range(2):
                total = (
                    part[2 * half, at - 1 : at - 1 + wide]
                    + part[2 * half + 1, at : at + wide]
                    + part[4 + half, at + 1 : at + 1 + wide]
                )
                low = base + GROUP * group + 2 * half
                keep = in_image
                if low < 0 or low + 2 > disps:
                    keep = keep & (lane_disp >= -low) & (lane_disp < disps - low)
                total = jnp.where(keep, jnp.maximum(total, 0.0), 0.0)
                high = total.astype(jnp.bfloat16)
                rest = (total - high.astype(jnp.float32)).astype(jnp.bfloat16)
                lane = 2 * SLAB * half
                target[here, lane : lane + SLAB] = high
                target[here, lane + SLAB : lane + 2 * SLAB] = rest
                if half == 0 and group > 0:
                    target[before, 4 * SLAB : 5 * SLAB] = high
                    target[before, 5 * SLAB : 6 * SLAB] = rest

    send_told(3)
    send_told(-1)
    receive_near()
    receive_far()
    permute(0, held_rows)
    volume(1, groups_d)
    waiting = []

    def step(layer, start, stop):
        products(layer, start, stop)
        if waiting:
            finish_layer(*waiting.pop())
        waiting.append((layer, start, stop))

    bounds = (0, 9, groups_d)
    for layer in range(MID + 1):
        lower = [max(0, b - layer) if b < groups_d else b for b in bounds]
        for start, stop in zip(lower, lower[1:]):
            step(layer, start, stop)
    finish_layer(*waiting.pop())

    per = SLAB // wide
    lane = lax.broadcasted_iota(jnp.int32, (8, SLAB), 1)
    place = lax.broadcasted_iota(jnp.int32, (8, SLAB), 0)
    within = lane // wide
    costs = []
    valids = []
    for first in range(0, groups_d - 1, per):
        taken = a_ref[MID + 1, first * wide : first * wide + SLAB]
        parts = across(line_ref[...], taken)
        cost = (
            pltpu.roll(parts[0:8], 1, 1) + parts[8:16] + pltpu.roll(parts[16:24], SLAB - 1, 1)
        )
        valid = (place < GROUP) & (within < min(per, groups_d - 1 - first))
        valids.append(valid)
        costs.append(jnp.where(valid, cost, -jnp.inf))
    def gathered(x, combine):
        return functools.reduce(
            combine, [x] + [pltpu.roll(x, SLAB - wide * k, 1) for k in range(1, per)]
        )

    top = jnp.max(functools.reduce(jnp.maximum, costs), axis=0, keepdims=True)
    top = gathered(jnp.broadcast_to(top, (8, SLAB)), jnp.maximum)
    tops = top
    for k in range(1, per):
        tops = jnp.where(within == k, pltpu.roll(top, wide * k, 1), tops)
    weight_sum = jnp.zeros((8, SLAB), jnp.float32)
    level_sum = jnp.zeros((8, SLAB), jnp.float32)
    for number, cost in enumerate(costs):
        weight = jnp.where(valids[number], jnp.exp(cost - tops), 0.0)
        level = GROUP * (number * per + within) + place
        weight_sum += weight
        level_sum += weight * (level.astype(jnp.float32) * (1.0 / disps))
    weight_sum = gathered(jnp.broadcast_to(jnp.sum(weight_sum, axis=0, keepdims=True), (8, SLAB)), jnp.add)
    level_sum = gathered(jnp.broadcast_to(jnp.sum(level_sum, axis=0, keepdims=True), (8, SLAB)), jnp.add)
    line = pltpu.roll(level_sum / weight_sum, SLAB - HALO, 1)
    out_ref[...] = line[0:1, 0:width_here]
    finish()


def window_shards(left_feat, right_feat, conv_first, conv_mid, conv_last):
    width = left_feat.shape[1]
    channels = left_feat.shape[2]
    groups = conv_first.shape[2]
    disps = DDEV * lax.axis_size("disp")
    width_all = width * lax.axis_size("disp") * lax.axis_size("cols")
    near, far, _, _, held_rows = exchange_plan(width)
    count = len(near) + len(far)
    wide = width + 2 * HALO
    rows = (disps // GROUP + 1) * wide
    size = channels // groups
    return pl.pallas_call(
        functools.partial(whole_kernel, disps, width_all),
        out_shape=pltpu.VMEM((1, width), jnp.float32),
        in_specs=[pl.BlockSpec(memory_space=pltpu.HBM)] * 5,
        out_specs=pl.BlockSpec(memory_space=pltpu.VMEM),
        scratch_shapes=[
            pltpu.VMEM((2, held_rows // BLOCK, BLOCK, channels), jnp.bfloat16),
            pltpu.SemaphoreType.DMA((count,)),
            pltpu.SemaphoreType.DMA((count,)),
            pltpu.SemaphoreType.DMA((2,)),
            pltpu.SemaphoreType.REGULAR((4,)),
            pltpu.SemaphoreType.DMA((3,)),
            pltpu.VMEM((2 * channels, size * SLAB), jnp.bfloat16),
            pltpu.VMEM(conv_first.shape, jnp.bfloat16),
            pltpu.VMEM(conv_mid.shape, jnp.bfloat16),
            pltpu.VMEM((27, conv_last.shape[2]), jnp.bfloat16),
            pltpu.VMEM((MID + 2, rows + 2 * wide, 6 * SLAB), jnp.bfloat16),
            pltpu.VMEM((MID + 1, 6, rows + 16, SLAB), jnp.float32),
            pltpu.VMEM((size, held_rows, SLAB), jnp.float32),
            pltpu.VMEM((MID + 1, 2 * SLAB, 4 * SLAB), jnp.bfloat16),
            pltpu.VMEM((MID + 1, 2 * SLAB, 6 * SLAB), jnp.bfloat16),
            pltpu.VMEM((32, 6 * SLAB), jnp.bfloat16),
            pltpu.VMEM((MID + 1, 4 * SLAB, 2 * SLAB), jnp.bfloat16),
            pltpu.VMEM((MID + 1, 6 * SLAB, 2 * SLAB), jnp.bfloat16),
        ],
        compiler_params=pltpu.CompilerParams(
            vmem_limit_bytes=56 * 1024 * 1024, collective_id=0, has_side_effects=True
        ),
    )(
        left_feat.reshape(-1, BLOCK, channels),
        right_feat.reshape(-1, BLOCK, channels),
        conv_first,
        conv_mid,
        conv_last.reshape(27, -1),
    )


def solution(mesh):
    rows, pieces = mesh.shape["rows"], mesh.shape["cols"] * mesh.shape["disp"]
    body = window_shards if rows == 2 and mesh.shape["disp"] == 4 and pieces == 8 else shards
    return jax.shard_map(
        body,
        mesh=mesh,
        in_specs=(
            P(("tiles", "rows"), ("cols", "disp"), None),
            P(("tiles", "rows"), ("cols", "disp"), None),
            P(),
            P(),
            P(),
        ),
        out_specs=P(("tiles", "rows"), ("cols", "disp")),
        check_vma=False,
    )
```

```python
import functools

import jax
import jax.numpy as jnp
from jax import lax
from jax.experimental import pallas as pl
from jax.experimental.pallas import tpu as pltpu
from jax.sharding import PartitionSpec as P

MID = 2
DDEV = 16


def extended_2(block, sides, width):
    for axis, dim in sides:
        count = lax.axis_size(axis)
        forward = [(i, i + 1) for i in range(count - 1)]
        backward = [(target, source) for source, target in forward]
        low = lax.ppermute(
            lax.slice_in_dim(block, block.shape[dim] - width, None, axis=dim), axis, forward
        )
        high = lax.ppermute(lax.slice_in_dim(block, 0, width, axis=dim), axis, backward)
        block = jnp.concatenate([low, block, high], axis=dim)
    return block


def passed_along(x, axis, by):
    peers = lax.axis_size(axis)
    pairs = [(i, i + by) for i in range(peers) if 0 <= i + by < peers]
    return lax.ppermute(x, axis, pairs)


def combined_all(part, axis, combine):
    gathered = jax.tree.map(lambda a: lax.all_gather(a, axis), part)

    def take(source):
        return jax.tree.map(lambda a: lax.dynamic_index_in_dim(a, source, 0, False), gathered)

    return lax.fori_loop(
        1, lax.axis_size(axis), lambda source, state: combine(state, take(source)), take(0)
    )


def correlate(left_full, extended, groups, first_disp, count, total_disp):
    rows_here, width_here, channels = left_full.shape
    group_size = channels // groups
    left_groups = left_full.reshape(rows_here, width_here, groups, group_size)

    def single(offset):
        disp_value = first_disp + offset
        shifted = lax.dynamic_slice_in_dim(extended, 2 * width_here - disp_value, width_here, 1)
        right_groups = shifted.reshape(rows_here, width_here, groups, group_size)
        corr = (
            jnp.einsum(
                "hwgc,hwgc->ghw", left_groups, right_groups, preferred_element_type=jnp.float32
            )
            / group_size
        )
        inside = (disp_value >= 0) & (disp_value < total_disp)
        return jnp.where(inside, corr, 0.0).astype(jnp.bfloat16)

    return lax.map(single, jnp.arange(count, dtype=jnp.int32))


def convolve(padded, kernel):
    depth_out = padded.shape[0] - 2
    in_chans = padded.shape[1]
    rows_out = padded.shape[2] - 2
    cols_out = padded.shape[3] - 2
    out_chans = kernel.shape[1]
    columns = jnp.concatenate(
        [
            padded[:, :, row_tap : row_tap + rows_out, col_tap : col_tap + cols_out]
            for row_tap in range(3)
            for col_tap in range(3)
        ],
        axis=1,
    )
    flat = columns.reshape(depth_out + 2, 9 * in_chans, rows_out * cols_out)
    summed = jnp.zeros((depth_out, out_chans, rows_out * cols_out), jnp.float32)
    for disp_tap in range(3):
        taps = (
            jnp.transpose(kernel[9 * disp_tap : 9 * disp_tap + 9], (1, 0, 2))
            .reshape(out_chans, 9 * in_chans)
            .astype(flat.dtype)
        )
        summed = summed + jnp.einsum(
            "ok,dkn->don",
            taps,
            flat[disp_tap : disp_tap + depth_out],
            preferred_element_type=jnp.float32,
            precision=lax.Precision.HIGHEST,
        )
    return summed.reshape(depth_out, out_chans, rows_out, cols_out)


def widen(hidden):
    return extended_2(hidden, (("disp", 0), ("rows", 2), ("cols", 3)), 1)


def combine_parts(earlier, later):
    highest = jnp.maximum(earlier[0], later[0])
    scale_one = jnp.exp(earlier[0] - highest)
    scale_two = jnp.exp(later[0] - highest)
    return (
        highest,
        earlier[1] * scale_one + later[1] * scale_two,
        earlier[2] * scale_one + later[2] * scale_two,
    )


def shards(left_feat, right_feat, conv_first, conv_mid, conv_last):
    piece_width = left_feat.shape[1]
    groups = conv_first.shape[2]
    disp_count = lax.axis_size("disp")
    depth_here = DDEV
    total_disp = depth_here * disp_count
    first_disp = lax.axis_index("disp") * depth_here
    left_full, right_full = (
        lax.all_gather(left_feat, "disp", axis=1, tiled=True),
        lax.all_gather(right_feat, "disp", axis=1, tiled=True),
    )
    prior_full = passed_along(right_full, "cols", 1)
    extended = jnp.concatenate([jnp.zeros_like(right_full), prior_full, right_full], axis=1)
    volume = correlate(left_full, extended, groups, first_disp, depth_here, total_disp)
    padded = extended_2(volume, (("disp", 0), ("rows", 2), ("cols", 3)), 1)
    hidden = jax.nn.relu(convolve(padded, conv_first))
    for layer in range(MID):
        hidden = jax.nn.relu(convolve(widen(hidden), conv_mid[layer]))
    cost_cube = convolve(widen(hidden), conv_last)[:, 0]
    levels = (
        (first_disp + jnp.arange(depth_here, dtype=jnp.int32)).astype(jnp.float32) / total_disp
    )[:, None, None]
    local_high = jnp.max(cost_cube, axis=0)
    weights = jnp.exp(cost_cube - local_high[None])
    merged = combined_all(
        (local_high, jnp.sum(weights, axis=0), jnp.sum(weights * levels, axis=0)),
        "disp",
        combine_parts,
    )
    whole_row = merged[2] / merged[1]
    return lax.dynamic_slice_in_dim(whole_row, lax.axis_index("disp") * piece_width, piece_width, 1)


HALO = 4
GROUP = 4
EDGE = 8
BLOCK = 8
SLAB = 128


def build_permutation(perm_ref, channels, groups):
    size = channels // groups
    rows, lanes = perm_ref.shape
    part = rows // 2
    lane = lax.broadcasted_iota(jnp.int32, (1, lanes), 1)
    group = lane % 64
    for row in range(2):
        wanted = group * size + lane // SLAB
        wanted = jnp.where((group < groups) & ((lane // 64) % 2 == row), wanted, -1)
        channel = lax.broadcasted_iota(jnp.int32, (part, lanes), 0)
        block = (channel == wanted).astype(jnp.float32).astype(jnp.bfloat16)
        perm_ref[row * part : (row + 1) * part, :] = block


def tap_of(a, r_in, r_out, e):
    return 9 * a + 3 * (r_in - r_out + 1) + e


def place_first(target, at, lead, slabs):
    for a, slab in enumerate(slabs):
        lane = SLAB * (lead + a)
        target[at : at + slab.shape[0], lane : lane + SLAB] = slab


def build_first(taps_ref, pair_ref, quad_ref):
    pair_ref[...] = jnp.zeros_like(pair_ref)
    quad_ref[...] = jnp.zeros_like(quad_ref)
    outs, ins = taps_ref.shape[1:]
    blank = jnp.zeros((outs, 64 - ins), jnp.float32)
    for e in range(3):
        for r_out in range(2):
            slabs = []
            for a in range(3):
                parts = []
                for r_in in range(2):
                    parts += [taps_ref[tap_of(a, r_in, r_out, e)].astype(jnp.float32), blank]
                slabs.append(jnp.concatenate(parts, axis=1).astype(jnp.bfloat16))
            if e < 2:
                for d_out in range(2):
                    place_first(pair_ref, e * 128 + d_out * 64 + r_out * 32, d_out, slabs)
            else:
                for d_out in range(GROUP):
                    place_first(quad_ref, d_out * 64 + r_out * 32, d_out, slabs)


def place_mid(target, at, lead, block):
    for half in range(2):
        piece = block[:, SLAB * half : SLAB * half + SLAB]
        for copy in range(2):
            lane = 2 * SLAB * (lead + half) + SLAB * copy
            target[at : at + piece.shape[0], lane : lane + SLAB] = piece


def build_mid(taps_ref, pair_ref, quad_ref):
    pair_ref[...] = jnp.zeros_like(pair_ref)
    quad_ref[...] = jnp.zeros_like(quad_ref)
    outs = taps_ref.shape[1]
    blank = jnp.zeros((outs, 64), jnp.float32)
    for e in range(3):
        for r_out in range(2):
            slabs = [
                taps_ref[tap_of(a, r_in, r_out, e)].astype(jnp.float32)
                for a in range(3)
                for r_in in range(2)
            ]
            shifted = (
                jnp.concatenate(slabs + [blank], axis=1).astype(jnp.bfloat16),
                jnp.concatenate([blank] + slabs, axis=1).astype(jnp.bfloat16),
            )
            if e < 2:
                for d_out in range(2):
                    place_mid(pair_ref, e * 128 + d_out * 64 + r_out * 32, 0, shifted[d_out])
            else:
                for d_out in range(GROUP):
                    place_mid(
                        quad_ref, d_out * 64 + r_out * 32, d_out // 2, shifted[d_out % 2]
                    )


def build_last(taps_ref, line_ref, row):
    taps = taps_ref[...].astype(jnp.float32)
    lines = []
    for e in range(3):
        for d_out in range(GROUP):
            parts = []
            for a in range(3):
                for r_in in range(2):
                    upper, lower = (tap_of(a, r_in, r_out, e) for r_out in range(2))
                    parts.append(
                        jnp.where(row == 0, taps[upper : upper + 1], taps[lower : lower + 1])
                    )
            if d_out > 0:
                parts.insert(0, jnp.zeros((1, 64 * d_out), jnp.float32))
            if d_out < GROUP - 1:
                parts.append(jnp.zeros((1, 64 * (GROUP - 1 - d_out)), jnp.float32))
            lines.append(jnp.concatenate(parts, axis=1))
        lines.append(jnp.zeros((8 - GROUP, 3 * SLAB), jnp.float32))
    lines.append(jnp.zeros((8, 3 * SLAB), jnp.float32))
    block = jnp.concatenate(lines, axis=0).astype(jnp.bfloat16)
    for pair in range(3):
        piece = block[:, SLAB * pair : SLAB * pair + SLAB]
        for copy in range(2):
            lane = SLAB * (2 * pair + copy)
            line_ref[:, lane : lane + SLAB] = piece


def across(x, banded):
    return lax.dot_general(
        x, banded, (((1,), (1,)), ((), ())), preferred_element_type=jnp.float32
    )


def exchange_plan(width):
    own = EDGE + 2 * width
    left_at = own + width + EDGE
    near = []
    for other in (1, 0):
        near.append((1, -1, other, 0, own + width, EDGE))
        near.append((0, -1, other, 0, left_at + EDGE + width, EDGE))
    near.append((1, 0, 1, 0, own, width))
    near.append((0, 0, 1, 0, left_at + EDGE, width))
    for other in (1, 0):
        near.append((1, 1, other, 0, own - width, width))
        near.append((0, 1, other, width - EDGE, left_at, EDGE))
    far = [(1, 2, other, 0, own - 2 * width, width) for other in (1, 0)]
    far += [(1, 3, other, width - EDGE, 0, EDGE) for other in (1, 0)]
    return tuple(near), tuple(far), own, left_at, left_at + width + 2 * EDGE


def exchange_steps(left_ref, right_ref, held, send_sem, recv_sem, own_sem, told_sem):
    width = left_ref.shape[0] * BLOCK
    near, far, own, left_at, _ = exchange_plan(width)
    copies = near + far
    row, col, disp = lax.axis_index("rows"), lax.axis_index("cols"), lax.axis_index("disp")
    col_disps = lax.axis_size("disp")
    pieces = col_disps * lax.axis_size("cols")
    piece = col * col_disps + disp
    barrier = pltpu.get_barrier_semaphore()
    reach = max(abs(by) for _, by, _, _, _, _ in copies)
    steps = sorted({by for _, by, _, _, _, _ in copies if by})
    related = [by for by in range(-reach, reach + 1) if by]

    def device(other, by):
        target = piece + by
        target_col = (target >= col_disps).astype(jnp.int32)
        return {
            "tiles": lax.axis_index("tiles"),
            "disp": target - col_disps * target_col,
            "rows": 1 - row if other else row,
            "cols": target_col,
        }

    def exists(by):
        return (piece + by >= 0) & (piece + by < pieces)

    def stays(by):
        return (disp + by >= 0) & (disp + by < col_disps)

    def lower(by):
        return stays(by) if by < 0 else exists(by) & (disp + by >= col_disps)

    def higher(by):
        return stays(by) if by > 0 else exists(by) & (disp + by < 0)

    def landing(target, count):
        return held.at[row, pl.ds(target // BLOCK, count // BLOCK)]

    def copy(number):
        view, by, other, source, target, count = copies[number]
        return pltpu.make_async_remote_copy(
            src_ref=landing((own if view else left_at + EDGE) + source, count),
            dst_ref=landing(target, count),
            send_sem=send_sem.at[number],
            recv_sem=recv_sem.at[number],
            device_id=device(other, by),
            device_id_type=pl.DeviceIdType.MESH,
        )

    own_loads = [
        pltpu.make_async_copy(source, landing(target, width), own_sem.at[number])
        for number, (source, target) in enumerate(
            ((left_ref, left_at + EDGE), (right_ref, own))
        )
    ]

    def tell(semaphore, by, other):
        pl.semaphore_signal(
            semaphore, inc=1, device_id=device(other, by), device_id_type=pl.DeviceIdType.MESH
        )

    def greet():
        for load in own_loads:
            load.start()
        edges = [0]
        for at in (own, left_at + EDGE):
            edges += [at // BLOCK, (at + width) // BLOCK]
        edges.append(held.shape[1])
        for first, last in zip(edges[::2], edges[1::2]):
            held[:, first:last] = jnp.zeros((2, last - first, BLOCK, held.shape[3]), held.dtype)
        tell(barrier, 0, 1)
        for by in related:

            @pl.when(higher(by))
            def _():
                for other in range(2):
                    tell(barrier, by, other)

    def start(by):
        for number, (_, step, _, _, _, _) in enumerate(copies):
            if step == by:
                copy(number).start()

    def meet():
        count = jnp.int32(1)
        for by in related:
            count = count + 2 * lower(by).astype(jnp.int32)
        pl.semaphore_wait(barrier, count)
        for by in steps:

            @pl.when(lower(-by))
            def _():
                for other in range(2):
                    tell(told_sem.at[steps.index(by)], -by, other)

        for load in own_loads:
            load.wait()

    def send(by):
        if by == 0:
            start(by)
        else:

            @pl.when(lower(by))
            def _():
                start(by)

    def send_told(by):
        @pl.when(higher(by))
        def _():
            pl.semaphore_wait(told_sem.at[steps.index(by)], 2)
            start(by)

    def receive(numbers):
        for number in numbers:

            @pl.when(exists(-copies[number][1]))
            def _():
                copy(number).wait_recv()

    def receive_near():
        receive(range(len(near)))

    def receive_far():
        receive(range(len(near), len(copies)))

    def finish():
        for number in range(len(copies)):

            @pl.when(exists(copies[number][1]))
            def _():
                copy(number).wait_send()

    return greet, meet, send, send_told, receive_near, receive_far, finish


def whole_kernel(
    disps,
    width_all,
    left_ref,
    right_ref,
    first_hbm,
    mid_hbm,
    last_hbm,
    out_ref,
    feat_ref,
    send_sem,
    recv_sem,
    own_sem,
    told_sem,
    load_sem,
    perm_ref,
    first_taps,
    mid_taps,
    last_taps,
    a_ref,
    p_ref,
    f_ref,
    pair_ref,
    quad_ref,
    line_ref,
    kpair_ref,
    kquad_ref,
):
    width_here = out_ref.shape[1]
    wide = width_here + 2 * HALO
    groups_d = disps // GROUP + 1
    channels, groups = left_ref.shape[2], first_taps.shape[2]
    size = channels // groups
    _, _, own, left_at, held_rows = exchange_plan(width_here)
    greet, meet, send, send_told, receive_near, receive_far, finish = exchange_steps(
        left_ref, right_ref, feat_ref, send_sem, recv_sem, own_sem, told_sem
    )
    loads = [
        pltpu.make_async_copy(source, target, load_sem.at[number])
        for number, (source, target) in enumerate(
            ((first_hbm, first_taps), (mid_hbm, mid_taps), (last_hbm, last_taps))
        )
    ]
    greet()
    for load in loads:
        load.start()
    meet()
    for by in (1, 0, 2, 3, -1):
        send(by)
    build_permutation(perm_ref, channels, groups)
    send_told(1)
    a_ref[0, 0:wide, :] = jnp.zeros((wide, 6 * SLAB), jnp.bfloat16)
    for layer in range(MID + 2):
        a_ref[layer, (groups_d - 1) * wide : groups_d * wide, 4 * SLAB :] = jnp.zeros(
            (wide, 2 * SLAB), jnp.bfloat16
        )
    loads[0].wait()
    build_first(first_taps, pair_ref.at[0], quad_ref.at[0])
    send_told(2)
    loads[1].wait()
    for layer in range(MID):
        build_mid(mid_taps.at[layer], pair_ref.at[layer + 1], quad_ref.at[layer + 1])
    loads[2].wait()
    for layer in range(MID + 1):
        kpair_ref[layer] = pair_ref[layer].T
        kquad_ref[layer] = quad_ref[layer].T
    build_last(last_taps, line_ref, lax.axis_index("rows"))

    def permute(start, stop):
        held = [
            feat_ref[row, start // BLOCK : stop // BLOCK].reshape(stop - start, channels)
            for row in range(2)
        ]
        for at in range(0, size * SLAB, 2 * SLAB):
            lanes = slice(at, at + 2 * SLAB)
            both = jnp.dot(
                held[0],
                perm_ref[0:channels, lanes],
                preferred_element_type=jnp.float32,
            ) + jnp.dot(
                held[1],
                perm_ref[channels : 2 * channels, lanes],
                preferred_element_type=jnp.float32,
            )
            f_ref[at // SLAB, start:stop] = both[:, :SLAB]
            f_ref[at // SLAB + 1, start:stop] = both[:, SLAB:]

    def volume(start, stop):
        for group in range(start, stop):
            sums = [None] * GROUP
            for k in range(size):
                left = f_ref[k, left_at + EDGE - HALO : left_at + EDGE - HALO + wide]
                for place in range(GROUP):
                    at = own - HALO - (GROUP * (group - 1) + place)
                    term = left * f_ref[k, at : at + wide]
                    sums[place] = term if k == 0 else sums[place] + term
            for place in range(GROUP):
                slab = (sums[place] / size).astype(jnp.bfloat16)
                here = slice(group * wide, (group + 1) * wide)
                a_ref[0, here, SLAB * place : SLAB * place + SLAB] = slab
                if place < 2:
                    before = slice((group - 1) * wide, group * wide)
                    lane = SLAB * (GROUP + place)
                    a_ref[0, before, lane : lane + SLAB] = slab

    piece = lax.axis_index("cols") * lax.axis_size("disp") + lax.axis_index("disp")
    column = piece * width_here - HALO + lax.broadcasted_iota(jnp.int32, (wide, SLAB), 0)
    in_image = (column >= 0) & (column < width_all)
    lane_disp = lax.broadcasted_iota(jnp.int32, (wide, SLAB), 1) // 64

    def products(layer, start, stop):
        source, part = a_ref.at[layer], p_ref.at[layer]
        middle = (start + stop) // 2

        def multiply(slab, first, last, lanes, taps_ref):
            rows = slice(first * wide, last * wide)
            got = jnp.dot(source[rows, lanes], taps_ref[layer], preferred_element_type=jnp.float32)
            held = slice(8 + first * wide, 8 + last * wide)
            part[slab, held] = got[:, :SLAB]
            part[slab + 1, held] = got[:, SLAB:]

        multiply(0, start, stop, slice(0, 4 * SLAB), kpair_ref)
        multiply(2, start, stop, slice(2 * SLAB, 6 * SLAB), kpair_ref)
        multiply(4, start, middle, slice(0, 6 * SLAB), kquad_ref)
        multiply(4, middle, stop, slice(0, 6 * SLAB), kquad_ref)

    def finish_layer(layer, start, stop):
        target, part = a_ref.at[layer + 1], p_ref.at[layer]
        base = layer + 1 - HALO
        for group in range(start, stop):
            at = 8 + group * wide
            here = slice(group * wide, (group + 1) * wide)
            before = slice((group - 1) * wide, group * wide)
            for half in range(2):
                total = (
                    part[2 * half, at - 1 : at - 1 + wide]
                    + part[2 * half + 1, at : at + wide]
                    + part[4 + half, at + 1 : at + 1 + wide]
                )
                low = base + GROUP * group + 2 * half
                keep = in_image
                if low < 0 or low + 2 > disps:
                    keep = keep & (lane_disp >= -low) & (lane_disp < disps - low)
                total = jnp.where(keep, jnp.maximum(total, 0.0), 0.0)
                high = total.astype(jnp.bfloat16)
                rest = (total - high.astype(jnp.float32)).astype(jnp.bfloat16)
                lane = 2 * SLAB * half
                target[here, lane : lane + SLAB] = high
                target[here, lane + SLAB : lane + 2 * SLAB] = rest
                if half == 0 and group > 0:
                    target[before, 4 * SLAB : 5 * SLAB] = high
                    target[before, 5 * SLAB : 6 * SLAB] = rest

    send_told(3)
    send_told(-1)
    far_rows = own - width_here
    receive_near()
    permute(far_rows, held_rows)
    volume(1, 8)
    receive_far()
    permute(0, far_rows)
    volume(8, groups_d)
    waiting = []

    def step(layer, start, stop):
        products(layer, start, stop)
        if waiting:
            finish_layer(*waiting.pop())
        waiting.append((layer, start, stop))

    for layer, bounds in enumerate(((0, 9, groups_d), (0, 8, groups_d), (0, 7, groups_d))):
        for start, stop in zip(bounds, bounds[1:]):
            step(layer, start, stop)
    finish_layer(*waiting.pop())

    per = SLAB // wide
    lane = lax.broadcasted_iota(jnp.int32, (8, SLAB), 1)
    place = lax.broadcasted_iota(jnp.int32, (8, SLAB), 0)
    within = (lane + HALO) // wide
    firsts = list(range(0, groups_d - 1, per))
    lowest = jnp.finfo(jnp.float32).min
    costs = []
    valids = []
    for begin in range(0, len(firsts), 2):
        some = firsts[begin : begin + 2]
        taken = [a_ref[MID + 1, first * wide : first * wide + SLAB] for first in some]
        joined = across(line_ref[...], jnp.concatenate(taken, axis=0))
        for number, first in enumerate(some):
            parts = joined[:, SLAB * number : SLAB * number + SLAB]
            cost = (
                pltpu.roll(parts[0:8], SLAB + 1 - HALO, 1)
                + pltpu.roll(parts[8:16], SLAB - HALO, 1)
                + pltpu.roll(parts[16:24], SLAB - 1 - HALO, 1)
            )
            valid = (place < GROUP) & (within < min(per, groups_d - 1 - first))
            valids.append(valid)
            costs.append(jnp.where(valid, cost, lowest))
    tops = functools.reduce(jnp.maximum, costs)
    weight_sum = jnp.zeros((8, SLAB), jnp.float32)
    level_sum = jnp.zeros((8, SLAB), jnp.float32)
    for number, cost in enumerate(costs):
        weight = jnp.where(valids[number], jnp.exp(cost - tops), 0.0)
        level = GROUP * (number * per + within) + place
        weight_sum += weight
        level_sum += weight * (level.astype(jnp.float32) * (1.0 / disps))

    def spread(x):
        return [x] + [pltpu.roll(x, SLAB - wide * k, 1) for k in range(1, per)]

    def merged(scales, x):
        return functools.reduce(jnp.add, [a * b for a, b in zip(scales, spread(x))])

    top = jnp.broadcast_to(jnp.max(tops, axis=0, keepdims=True), (8, SLAB))
    scale = jnp.exp(tops - top)
    weight_sum = jnp.broadcast_to(jnp.sum(weight_sum * scale, axis=0, keepdims=True), (8, SLAB))
    level_sum = jnp.broadcast_to(jnp.sum(level_sum * scale, axis=0, keepdims=True), (8, SLAB))
    around = spread(top)
    highest = functools.reduce(jnp.maximum, around)
    scales = [jnp.exp(one - highest) for one in around]
    line = merged(scales, level_sum) / merged(scales, weight_sum)
    out_ref[...] = line[0:1, 0:width_here]
    finish()


def window_shards(left_feat, right_feat, conv_first, conv_mid, conv_last):
    width = left_feat.shape[1]
    channels = left_feat.shape[2]
    groups = conv_first.shape[2]
    disps = DDEV * lax.axis_size("disp")
    width_all = width * lax.axis_size("disp") * lax.axis_size("cols")
    near, far, _, _, held_rows = exchange_plan(width)
    count = len(near) + len(far)
    wide = width + 2 * HALO
    rows = (disps // GROUP + 1) * wide
    size = channels // groups
    return pl.pallas_call(
        functools.partial(whole_kernel, disps, width_all),
        out_shape=pltpu.VMEM((1, width), jnp.float32),
        in_specs=[pl.BlockSpec(memory_space=pltpu.HBM)] * 5,
        out_specs=pl.BlockSpec(memory_space=pltpu.VMEM),
        scratch_shapes=[
            pltpu.VMEM((2, held_rows // BLOCK, BLOCK, channels), jnp.bfloat16),
            pltpu.SemaphoreType.DMA((count,)),
            pltpu.SemaphoreType.DMA((count,)),
            pltpu.SemaphoreType.DMA((2,)),
            pltpu.SemaphoreType.REGULAR((4,)),
            pltpu.SemaphoreType.DMA((3,)),
            pltpu.VMEM((2 * channels, size * SLAB), jnp.bfloat16),
            pltpu.VMEM(conv_first.shape, jnp.bfloat16),
            pltpu.VMEM(conv_mid.shape, jnp.bfloat16),
            pltpu.VMEM((27, conv_last.shape[2]), jnp.bfloat16),
            pltpu.VMEM((MID + 2, rows + 2 * wide, 6 * SLAB), jnp.bfloat16),
            pltpu.VMEM((MID + 1, 6, rows + 16, SLAB), jnp.float32),
            pltpu.VMEM((size, held_rows, SLAB), jnp.float32),
            pltpu.VMEM((MID + 1, 2 * SLAB, 4 * SLAB), jnp.bfloat16),
            pltpu.VMEM((MID + 1, 2 * SLAB, 6 * SLAB), jnp.bfloat16),
            pltpu.VMEM((32, 6 * SLAB), jnp.bfloat16),
            pltpu.VMEM((MID + 1, 4 * SLAB, 2 * SLAB), jnp.bfloat16),
            pltpu.VMEM((MID + 1, 6 * SLAB, 2 * SLAB), jnp.bfloat16),
        ],
        compiler_params=pltpu.CompilerParams(
            vmem_limit_bytes=56 * 1024 * 1024, collective_id=0, has_side_effects=True
        ),
    )(
        left_feat.reshape(-1, BLOCK, channels),
        right_feat.reshape(-1, BLOCK, channels),
        conv_first,
        conv_mid,
        conv_last.reshape(27, -1),
    )


def solution(mesh):
    rows, pieces = mesh.shape["rows"], mesh.shape["cols"] * mesh.shape["disp"]
    body = window_shards if rows == 2 and mesh.shape["disp"] == 4 and pieces == 8 else shards
    return jax.shard_map(
        body,
        mesh=mesh,
        in_specs=(
            P(("tiles", "rows"), ("cols", "disp"), None),
            P(("tiles", "rows"), ("cols", "disp"), None),
            P(),
            P(),
            P(),
        ),
        out_specs=P(("tiles", "rows"), ("cols", "disp")),
        check_vma=False,
    )
```

```python
import functools

import jax
import jax.numpy as jnp
from jax import lax
from jax.experimental import pallas as pl
from jax.experimental.pallas import tpu as pltpu
from jax.sharding import PartitionSpec as P

MID = 2
DDEV = 16


def extended_2(block, sides, width):
    for axis, dim in sides:
        count = lax.axis_size(axis)
        forward = [(i, i + 1) for i in range(count - 1)]
        backward = [(target, source) for source, target in forward]
        low = lax.ppermute(
            lax.slice_in_dim(block, block.shape[dim] - width, None, axis=dim), axis, forward
        )
        high = lax.ppermute(lax.slice_in_dim(block, 0, width, axis=dim), axis, backward)
        block = jnp.concatenate([low, block, high], axis=dim)
    return block


def passed_along(x, axis, by):
    peers = lax.axis_size(axis)
    pairs = [(i, i + by) for i in range(peers) if 0 <= i + by < peers]
    return lax.ppermute(x, axis, pairs)


def combined_all(part, axis, combine):
    gathered = jax.tree.map(lambda a: lax.all_gather(a, axis), part)

    def take(source):
        return jax.tree.map(lambda a: lax.dynamic_index_in_dim(a, source, 0, False), gathered)

    return lax.fori_loop(
        1, lax.axis_size(axis), lambda source, state: combine(state, take(source)), take(0)
    )


def correlate(left_full, extended, groups, first_disp, count, total_disp):
    rows_here, width_here, channels = left_full.shape
    group_size = channels // groups
    left_groups = left_full.reshape(rows_here, width_here, groups, group_size)

    def single(offset):
        disp_value = first_disp + offset
        shifted = lax.dynamic_slice_in_dim(extended, 2 * width_here - disp_value, width_here, 1)
        right_groups = shifted.reshape(rows_here, width_here, groups, group_size)
        corr = (
            jnp.einsum(
                "hwgc,hwgc->ghw", left_groups, right_groups, preferred_element_type=jnp.float32
            )
            / group_size
        )
        inside = (disp_value >= 0) & (disp_value < total_disp)
        return jnp.where(inside, corr, 0.0).astype(jnp.bfloat16)

    return lax.map(single, jnp.arange(count, dtype=jnp.int32))


def convolve(padded, kernel):
    depth_out = padded.shape[0] - 2
    in_chans = padded.shape[1]
    rows_out = padded.shape[2] - 2
    cols_out = padded.shape[3] - 2
    out_chans = kernel.shape[1]
    columns = jnp.concatenate(
        [
            padded[:, :, row_tap : row_tap + rows_out, col_tap : col_tap + cols_out]
            for row_tap in range(3)
            for col_tap in range(3)
        ],
        axis=1,
    )
    flat = columns.reshape(depth_out + 2, 9 * in_chans, rows_out * cols_out)
    summed = jnp.zeros((depth_out, out_chans, rows_out * cols_out), jnp.float32)
    for disp_tap in range(3):
        taps = (
            jnp.transpose(kernel[9 * disp_tap : 9 * disp_tap + 9], (1, 0, 2))
            .reshape(out_chans, 9 * in_chans)
            .astype(flat.dtype)
        )
        summed = summed + jnp.einsum(
            "ok,dkn->don",
            taps,
            flat[disp_tap : disp_tap + depth_out],
            preferred_element_type=jnp.float32,
            precision=lax.Precision.HIGHEST,
        )
    return summed.reshape(depth_out, out_chans, rows_out, cols_out)


def widen(hidden):
    return extended_2(hidden, (("disp", 0), ("rows", 2), ("cols", 3)), 1)


def combine_parts(earlier, later):
    highest = jnp.maximum(earlier[0], later[0])
    scale_one = jnp.exp(earlier[0] - highest)
    scale_two = jnp.exp(later[0] - highest)
    return (
        highest,
        earlier[1] * scale_one + later[1] * scale_two,
        earlier[2] * scale_one + later[2] * scale_two,
    )


def shards(left_feat, right_feat, conv_first, conv_mid, conv_last):
    piece_width = left_feat.shape[1]
    groups = conv_first.shape[2]
    disp_count = lax.axis_size("disp")
    depth_here = DDEV
    total_disp = depth_here * disp_count
    first_disp = lax.axis_index("disp") * depth_here
    left_full, right_full = (
        lax.all_gather(left_feat, "disp", axis=1, tiled=True),
        lax.all_gather(right_feat, "disp", axis=1, tiled=True),
    )
    prior_full = passed_along(right_full, "cols", 1)
    extended = jnp.concatenate([jnp.zeros_like(right_full), prior_full, right_full], axis=1)
    volume = correlate(left_full, extended, groups, first_disp, depth_here, total_disp)
    padded = extended_2(volume, (("disp", 0), ("rows", 2), ("cols", 3)), 1)
    hidden = jax.nn.relu(convolve(padded, conv_first))
    for layer in range(MID):
        hidden = jax.nn.relu(convolve(widen(hidden), conv_mid[layer]))
    cost_cube = convolve(widen(hidden), conv_last)[:, 0]
    levels = (
        (first_disp + jnp.arange(depth_here, dtype=jnp.int32)).astype(jnp.float32) / total_disp
    )[:, None, None]
    local_high = jnp.max(cost_cube, axis=0)
    weights = jnp.exp(cost_cube - local_high[None])
    merged = combined_all(
        (local_high, jnp.sum(weights, axis=0), jnp.sum(weights * levels, axis=0)),
        "disp",
        combine_parts,
    )
    whole_row = merged[2] / merged[1]
    return lax.dynamic_slice_in_dim(whole_row, lax.axis_index("disp") * piece_width, piece_width, 1)


HALO = 4
GROUP = 4
EDGE = 8
BLOCK = 8
SLAB = 128


def build_permutation(perm_ref, channels, groups):
    size = channels // groups
    rows, lanes = perm_ref.shape
    part = rows // 2
    lane = lax.broadcasted_iota(jnp.int32, (1, lanes), 1)
    group = lane % 64
    for row in range(2):
        wanted = group * size + lane // SLAB
        wanted = jnp.where((group < groups) & ((lane // 64) % 2 == row), wanted, -1)
        channel = lax.broadcasted_iota(jnp.int32, (part, lanes), 0)
        block = (channel == wanted).astype(jnp.float32).astype(jnp.bfloat16)
        perm_ref[row * part : (row + 1) * part, :] = block


def tap_of(a, r_in, r_out, e):
    return 9 * a + 3 * (r_in - r_out + 1) + e


def place_first(target, at, lead, slabs):
    for a, slab in enumerate(slabs):
        lane = SLAB * (lead + a)
        target[at : at + slab.shape[0], lane : lane + SLAB] = slab


def build_first(taps_ref, pair_ref, quad_ref):
    pair_ref[...] = jnp.zeros_like(pair_ref)
    quad_ref[...] = jnp.zeros_like(quad_ref)
    outs, ins = taps_ref.shape[1:]
    blank = jnp.zeros((outs, 64 - ins), jnp.float32)
    for e in range(3):
        for r_out in range(2):
            slabs = []
            for a in range(3):
                parts = []
                for r_in in range(2):
                    parts += [taps_ref[tap_of(a, r_in, r_out, e)].astype(jnp.float32), blank]
                slabs.append(jnp.concatenate(parts, axis=1).astype(jnp.bfloat16))
            if e < 2:
                for d_out in range(2):
                    place_first(pair_ref, e * 128 + d_out * 64 + r_out * 32, d_out, slabs)
            else:
                for d_out in range(GROUP):
                    place_first(quad_ref, d_out * 64 + r_out * 32, d_out, slabs)


def place_mid(target, at, lead, block):
    for half in range(2):
        piece = block[:, SLAB * half : SLAB * half + SLAB]
        for copy in range(2):
            lane = 2 * SLAB * (lead + half) + SLAB * copy
            target[at : at + piece.shape[0], lane : lane + SLAB] = piece


def build_mid(taps_ref, pair_ref, quad_ref):
    pair_ref[...] = jnp.zeros_like(pair_ref)
    quad_ref[...] = jnp.zeros_like(quad_ref)
    outs = taps_ref.shape[1]
    blank = jnp.zeros((outs, 64), jnp.float32)
    for e in range(3):
        for r_out in range(2):
            slabs = [
                taps_ref[tap_of(a, r_in, r_out, e)].astype(jnp.float32)
                for a in range(3)
                for r_in in range(2)
            ]
            shifted = (
                jnp.concatenate(slabs + [blank], axis=1).astype(jnp.bfloat16),
                jnp.concatenate([blank] + slabs, axis=1).astype(jnp.bfloat16),
            )
            if e < 2:
                for d_out in range(2):
                    place_mid(pair_ref, e * 128 + d_out * 64 + r_out * 32, 0, shifted[d_out])
            else:
                for d_out in range(GROUP):
                    place_mid(
                        quad_ref, d_out * 64 + r_out * 32, d_out // 2, shifted[d_out % 2]
                    )


def build_last(taps_ref, line_ref, row):
    taps = taps_ref[...].astype(jnp.float32)
    lines = []
    for e in range(3):
        for d_out in range(GROUP):
            parts = []
            for a in range(3):
                for r_in in range(2):
                    upper, lower = (tap_of(a, r_in, r_out, e) for r_out in range(2))
                    parts.append(
                        jnp.where(row == 0, taps[upper : upper + 1], taps[lower : lower + 1])
                    )
            if d_out > 0:
                parts.insert(0, jnp.zeros((1, 64 * d_out), jnp.float32))
            if d_out < GROUP - 1:
                parts.append(jnp.zeros((1, 64 * (GROUP - 1 - d_out)), jnp.float32))
            lines.append(jnp.concatenate(parts, axis=1))
        lines.append(jnp.zeros((8 - GROUP, 3 * SLAB), jnp.float32))
    lines.append(jnp.zeros((8, 3 * SLAB), jnp.float32))
    block = jnp.concatenate(lines, axis=0).astype(jnp.bfloat16)
    for pair in range(3):
        piece = block[:, SLAB * pair : SLAB * pair + SLAB]
        for copy in range(2):
            lane = SLAB * (2 * pair + copy)
            line_ref[:, lane : lane + SLAB] = piece


def across(x, banded):
    return lax.dot_general(
        x, banded, (((1,), (1,)), ((), ())), preferred_element_type=jnp.float32
    )


def exchange_plan(width):
    n = width // BLOCK
    near = [(-1, other, None, 3 * n + 1, 2) for other in (1, 0)]
    near.append((0, 1, 0, 0, 2 * n))
    near += [(1, other, n - 1, 2 * n, n + 1) for other in (1, 0)]
    far = [(2, other, n, 3 * n + 3, n) for other in (1, 0)]
    far += [(3, other, 2 * n - 1, 4 * n + 3, 1) for other in (1, 0)]
    right, left = n + n + 1, 3 * n + 3
    places = (
        (0, n, left),
        (n, n, right),
        (2 * n, 1, left - 1),
        (2 * n + 1, n, right - n),
        (3 * n + 1, 1, right + n),
        (3 * n + 2, 1, left + n),
        (3 * n + 3, n, right - 2 * n),
        (4 * n + 3, 1, 0),
    )
    own, left_at = right * BLOCK, (left - 1) * BLOCK
    return tuple(near), tuple(far), places, own, left_at, (4 * n + 4) * BLOCK


def exchange_steps(left_ref, right_ref, held, edge_ref, send_sem, recv_sem, own_sem, told_sem):
    width = left_ref.shape[0] * BLOCK
    blocks = width // BLOCK
    near, far, _, _, _, _ = exchange_plan(width)
    copies = near + far
    row, col, disp = lax.axis_index("rows"), lax.axis_index("cols"), lax.axis_index("disp")
    col_disps = lax.axis_size("disp")
    pieces = col_disps * lax.axis_size("cols")
    piece = col * col_disps + disp
    barrier = pltpu.get_barrier_semaphore()
    reach = max(abs(by) for by, _, _, _, _ in copies)
    steps = sorted({by for by, _, _, _, _ in copies if by})
    related = [by for by in range(-reach, reach + 1) if by]

    def device(other, by):
        target = piece + by
        target_col = (target >= col_disps).astype(jnp.int32)
        return {
            "tiles": lax.axis_index("tiles"),
            "disp": target - col_disps * target_col,
            "rows": 1 - row if other else row,
            "cols": target_col,
        }

    def exists(by):
        return (piece + by >= 0) & (piece + by < pieces)

    def stays(by):
        return (disp + by >= 0) & (disp + by < col_disps)

    def lower(by):
        return stays(by) if by < 0 else exists(by) & (disp + by >= col_disps)

    def higher(by):
        return stays(by) if by > 0 else exists(by) & (disp + by < 0)

    def copy(number):
        by, other, source, target, count = copies[number]
        return pltpu.make_async_remote_copy(
            src_ref=edge_ref if source is None else held.at[row, pl.ds(source, count)],
            dst_ref=held.at[row, pl.ds(target, count)],
            send_sem=send_sem.at[number],
            recv_sem=recv_sem.at[number],
            device_id=device(other, by),
            device_id_type=pl.DeviceIdType.MESH,
        )

    own_loads = [
        pltpu.make_async_copy(source, held.at[row, pl.ds(target, blocks)], own_sem.at[number])
        for number, (source, target) in enumerate(((left_ref, 0), (right_ref, blocks)))
    ]

    def tell(semaphore, by, other):
        pl.semaphore_signal(
            semaphore, inc=1, device_id=device(other, by), device_id_type=pl.DeviceIdType.MESH
        )

    def greet():
        for load in own_loads:
            load.start()
        empty = (2, held.shape[1] - 2 * blocks, BLOCK, held.shape[3])
        held[:, 2 * blocks :] = jnp.zeros(empty, held.dtype)
        tell(barrier, 0, 1)
        for by in related:

            @pl.when(higher(by))
            def _():
                for other in range(2):
                    tell(barrier, by, other)

    def start(by):
        for number, (step, _, _, _, _) in enumerate(copies):
            if step == by:
                copy(number).start()

    def meet():
        count = jnp.int32(1)
        for by in related:
            count = count + 2 * lower(by).astype(jnp.int32)
        pl.semaphore_wait(barrier, count)
        for by in steps:

            @pl.when(lower(-by))
            def _():
                for other in range(2):
                    tell(told_sem.at[steps.index(by)], -by, other)

        for load in own_loads:
            load.wait()
        edge_ref[0] = held[row, blocks]
        edge_ref[1] = held[row, 0]

    def send(by):
        if by == 0:
            start(by)
        else:

            @pl.when(lower(by))
            def _():
                start(by)

    def send_told(by):
        @pl.when(higher(by))
        def _():
            pl.semaphore_wait(told_sem.at[steps.index(by)], 2)
            start(by)

    def receive(numbers):
        for number in numbers:

            @pl.when(exists(-copies[number][0]))
            def _():
                copy(number).wait_recv()

    def receive_near():
        receive(range(len(near)))

    def receive_far():
        receive(range(len(near), len(copies)))

    def finish():
        for number in range(len(copies)):

            @pl.when(exists(copies[number][0]))
            def _():
                copy(number).wait_send()

    return greet, meet, send, send_told, receive_near, receive_far, finish


def whole_kernel(
    disps,
    width_all,
    left_ref,
    right_ref,
    first_hbm,
    mid_hbm,
    last_hbm,
    out_ref,
    feat_ref,
    edge_ref,
    send_sem,
    recv_sem,
    own_sem,
    told_sem,
    load_sem,
    perm_ref,
    first_taps,
    mid_taps,
    last_taps,
    a_ref,
    p_ref,
    f_ref,
    pair_ref,
    quad_ref,
    line_ref,
    kpair_ref,
    kquad_ref,
):
    width_here = out_ref.shape[1]
    wide = width_here + 2 * HALO
    groups_d = disps // GROUP + 1
    channels, groups = left_ref.shape[2], first_taps.shape[2]
    size = channels // groups
    _, _, places, own, left_at, held_rows = exchange_plan(width_here)
    greet, meet, send, send_told, receive_near, receive_far, finish = exchange_steps(
        left_ref, right_ref, feat_ref, edge_ref, send_sem, recv_sem, own_sem, told_sem
    )
    loads = [
        pltpu.make_async_copy(source, target, load_sem.at[number])
        for number, (source, target) in enumerate(
            ((first_hbm, first_taps), (mid_hbm, mid_taps), (last_hbm, last_taps))
        )
    ]
    greet()
    for load in loads:
        load.start()
    meet()
    for by in (1, 0, 2, 3, -1):
        send(by)
    build_permutation(perm_ref, channels, groups)
    send_told(1)
    a_ref[0, 0:wide, :] = jnp.zeros((wide, 6 * SLAB), jnp.bfloat16)
    for layer in range(MID + 2):
        a_ref[layer, (groups_d - 1) * wide : groups_d * wide, 4 * SLAB :] = jnp.zeros(
            (wide, 2 * SLAB), jnp.bfloat16
        )
    loads[0].wait()
    build_first(first_taps, pair_ref.at[0], quad_ref.at[0])
    send_told(2)
    loads[1].wait()
    for layer in range(MID):
        build_mid(mid_taps.at[layer], pair_ref.at[layer + 1], quad_ref.at[layer + 1])
    loads[2].wait()
    for layer in range(MID + 1):
        kpair_ref[layer] = pair_ref[layer].T
        kquad_ref[layer] = quad_ref[layer].T
    build_last(last_taps, line_ref, lax.axis_index("rows"))

    def permute(start, stop):
        held = [
            feat_ref[row, start // BLOCK : stop // BLOCK].reshape(stop - start, channels)
            for row in range(2)
        ]
        for at in range(0, size * SLAB, 2 * SLAB):
            lanes = slice(at, at + 2 * SLAB)
            both = jnp.dot(
                held[0],
                perm_ref[0:channels, lanes],
                preferred_element_type=jnp.float32,
            ) + jnp.dot(
                held[1],
                perm_ref[channels : 2 * channels, lanes],
                preferred_element_type=jnp.float32,
            )
            for first, count, place in places:
                begin, end, to = (BLOCK * x for x in (first, first + count, place))
                if start <= begin < stop:
                    rows, held_to = slice(begin - start, end - start), slice(to, to + end - begin)
                    f_ref[at // SLAB, held_to] = both[rows, :SLAB]
                    f_ref[at // SLAB + 1, held_to] = both[rows, SLAB:]

    def volume(start, stop):
        for group in range(start, stop):
            sums = [None] * GROUP
            for k in range(size):
                left = f_ref[k, left_at + EDGE - HALO : left_at + EDGE - HALO + wide]
                for place in range(GROUP):
                    at = own - HALO - (GROUP * (group - 1) + place)
                    term = left * f_ref[k, at : at + wide]
                    sums[place] = term if k == 0 else sums[place] + term
            for place in range(GROUP):
                slab = (sums[place] / size).astype(jnp.bfloat16)
                here = slice(group * wide, (group + 1) * wide)
                a_ref[0, here, SLAB * place : SLAB * place + SLAB] = slab
                if place < 2:
                    before = slice((group - 1) * wide, group * wide)
                    lane = SLAB * (GROUP + place)
                    a_ref[0, before, lane : lane + SLAB] = slab

    piece = lax.axis_index("cols") * lax.axis_size("disp") + lax.axis_index("disp")
    column = piece * width_here - HALO + lax.broadcasted_iota(jnp.int32, (wide, SLAB), 0)
    in_image = (column >= 0) & (column < width_all)
    lane_disp = lax.broadcasted_iota(jnp.int32, (wide, SLAB), 1) // 64

    def products(layer, start, stop):
        source, part = a_ref.at[layer], p_ref.at[layer]
        middle = (start + stop) // 2

        def multiply(slab, first, last, lanes, taps_ref):
            rows = slice(first * wide, last * wide)
            got = jnp.dot(source[rows, lanes], taps_ref[layer], preferred_element_type=jnp.float32)
            held = slice(8 + first * wide, 8 + last * wide)
            part[slab, held] = got[:, :SLAB]
            part[slab + 1, held] = got[:, SLAB:]

        multiply(0, start, stop, slice(0, 4 * SLAB), kpair_ref)
        multiply(2, start, stop, slice(2 * SLAB, 6 * SLAB), kpair_ref)
        multiply(4, start, middle, slice(0, 6 * SLAB), kquad_ref)
        multiply(4, middle, stop, slice(0, 6 * SLAB), kquad_ref)

    def finish_layer(layer, start, stop):
        target, part = a_ref.at[layer + 1], p_ref.at[layer]
        base = layer + 1 - HALO
        for group in range(start, stop):
            at = 8 + group * wide
            here = slice(group * wide, (group + 1) * wide)
            before = slice((group - 1) * wide, group * wide)
            for half in range(2):
                total = (
                    part[2 * half, at - 1 : at - 1 + wide]
                    + part[2 * half + 1, at : at + wide]
                    + part[4 + half, at + 1 : at + 1 + wide]
                )
                low = base + GROUP * group + 2 * half
                keep = in_image
                if low < 0 or low + 2 > disps:
                    keep = keep & (lane_disp >= -low) & (lane_disp < disps - low)
                total = jnp.where(keep, jnp.maximum(total, 0.0), 0.0)
                high = total.astype(jnp.bfloat16)
                rest = (total - high.astype(jnp.float32)).astype(jnp.bfloat16)
                lane = 2 * SLAB * half
                target[here, lane : lane + SLAB] = high
                target[here, lane + SLAB : lane + 2 * SLAB] = rest
                if half == 0 and group > 0:
                    target[before, 4 * SLAB : 5 * SLAB] = high
                    target[before, 5 * SLAB : 6 * SLAB] = rest

    send_told(3)
    send_told(-1)
    near_rows = held_rows - width_here - BLOCK
    receive_near()
    permute(0, near_rows)
    volume(1, 8)
    receive_far()
    permute(near_rows, held_rows)
    volume(8, groups_d)
    waiting = []

    def step(layer, start, stop):
        products(layer, start, stop)
        if waiting:
            finish_layer(*waiting.pop())
        waiting.append((layer, start, stop))

    for layer, bounds in enumerate(((0, 9, groups_d), (0, 8, groups_d), (0, 7, groups_d))):
        for start, stop in zip(bounds, bounds[1:]):
            step(layer, start, stop)
    finish_layer(*waiting.pop())

    per = SLAB // wide
    lane = lax.broadcasted_iota(jnp.int32, (8, SLAB), 1)
    place = lax.broadcasted_iota(jnp.int32, (8, SLAB), 0)
    within = (lane + HALO) // wide
    firsts = list(range(0, groups_d - 1, per))
    lowest = jnp.finfo(jnp.float32).min
    costs = []
    valids = []
    for begin in range(0, len(firsts), 2):
        some = firsts[begin : begin + 2]
        taken = [a_ref[MID + 1, first * wide : first * wide + SLAB] for first in some]
        joined = across(line_ref[...], jnp.concatenate(taken, axis=0))
        for number, first in enumerate(some):
            parts = joined[:, SLAB * number : SLAB * number + SLAB]
            cost = (
                pltpu.roll(parts[0:8], SLAB + 1 - HALO, 1)
                + pltpu.roll(parts[8:16], SLAB - HALO, 1)
                + pltpu.roll(parts[16:24], SLAB - 1 - HALO, 1)
            )
            valid = (place < GROUP) & (within < min(per, groups_d - 1 - first))
            valids.append(valid)
            costs.append(jnp.where(valid, cost, lowest))
    tops = functools.reduce(jnp.maximum, costs)
    weight_sum = jnp.zeros((8, SLAB), jnp.float32)
    level_sum = jnp.zeros((8, SLAB), jnp.float32)
    for number, cost in enumerate(costs):
        weight = jnp.where(valids[number], jnp.exp(cost - tops), 0.0)
        level = GROUP * (number * per + within) + place
        weight_sum += weight
        level_sum += weight * (level.astype(jnp.float32) * (1.0 / disps))

    def spread(x):
        return [x] + [pltpu.roll(x, SLAB - wide * k, 1) for k in range(1, per)]

    def merged(scales, x):
        return functools.reduce(jnp.add, [a * b for a, b in zip(scales, spread(x))])

    top = jnp.broadcast_to(jnp.max(tops, axis=0, keepdims=True), (8, SLAB))
    scale = jnp.exp(tops - top)
    weight_sum = jnp.broadcast_to(jnp.sum(weight_sum * scale, axis=0, keepdims=True), (8, SLAB))
    level_sum = jnp.broadcast_to(jnp.sum(level_sum * scale, axis=0, keepdims=True), (8, SLAB))
    around = spread(top)
    highest = functools.reduce(jnp.maximum, around)
    scales = [jnp.exp(one - highest) for one in around]
    line = merged(scales, level_sum) / merged(scales, weight_sum)
    out_ref[...] = line[0:1, 0:width_here]
    finish()


def window_shards(left_feat, right_feat, conv_first, conv_mid, conv_last):
    width = left_feat.shape[1]
    channels = left_feat.shape[2]
    groups = conv_first.shape[2]
    disps = DDEV * lax.axis_size("disp")
    width_all = width * lax.axis_size("disp") * lax.axis_size("cols")
    near, far, _, _, _, held_rows = exchange_plan(width)
    count = len(near) + len(far)
    wide = width + 2 * HALO
    rows = (disps // GROUP + 1) * wide
    size = channels // groups
    return pl.pallas_call(
        functools.partial(whole_kernel, disps, width_all),
        out_shape=pltpu.VMEM((1, width), jnp.float32),
        in_specs=[pl.BlockSpec(memory_space=pltpu.HBM)] * 5,
        out_specs=pl.BlockSpec(memory_space=pltpu.VMEM),
        scratch_shapes=[
            pltpu.VMEM((2, held_rows // BLOCK, BLOCK, channels), jnp.bfloat16),
            pltpu.VMEM((2, BLOCK, channels), jnp.bfloat16),
            pltpu.SemaphoreType.DMA((count,)),
            pltpu.SemaphoreType.DMA((count,)),
            pltpu.SemaphoreType.DMA((2,)),
            pltpu.SemaphoreType.REGULAR((4,)),
            pltpu.SemaphoreType.DMA((3,)),
            pltpu.VMEM((2 * channels, size * SLAB), jnp.bfloat16),
            pltpu.VMEM(conv_first.shape, jnp.bfloat16),
            pltpu.VMEM(conv_mid.shape, jnp.bfloat16),
            pltpu.VMEM((27, conv_last.shape[2]), jnp.bfloat16),
            pltpu.VMEM((MID + 2, rows + 2 * wide, 6 * SLAB), jnp.bfloat16),
            pltpu.VMEM((MID + 1, 6, rows + 16, SLAB), jnp.float32),
            pltpu.VMEM((size, held_rows, SLAB), jnp.float32),
            pltpu.VMEM((MID + 1, 2 * SLAB, 4 * SLAB), jnp.bfloat16),
            pltpu.VMEM((MID + 1, 2 * SLAB, 6 * SLAB), jnp.bfloat16),
            pltpu.VMEM((32, 6 * SLAB), jnp.bfloat16),
            pltpu.VMEM((MID + 1, 4 * SLAB, 2 * SLAB), jnp.bfloat16),
            pltpu.VMEM((MID + 1, 6 * SLAB, 2 * SLAB), jnp.bfloat16),
        ],
        compiler_params=pltpu.CompilerParams(
            vmem_limit_bytes=56 * 1024 * 1024, collective_id=0, has_side_effects=True
        ),
    )(
        left_feat.reshape(-1, BLOCK, channels),
        right_feat.reshape(-1, BLOCK, channels),
        conv_first,
        conv_mid,
        conv_last.reshape(27, -1),
    )


def solution(mesh):
    rows, pieces = mesh.shape["rows"], mesh.shape["cols"] * mesh.shape["disp"]
    body = window_shards if rows == 2 and mesh.shape["disp"] == 4 and pieces == 8 else shards
    return jax.shard_map(
        body,
        mesh=mesh,
        in_specs=(
            P(("tiles", "rows"), ("cols", "disp"), None),
            P(("tiles", "rows"), ("cols", "disp"), None),
            P(),
            P(),
            P(),
        ),
        out_specs=P(("tiles", "rows"), ("cols", "disp")),
        check_vma=False,
    )
```

```python
import functools

import jax
import jax.numpy as jnp
from jax import lax
from jax.experimental import pallas as pl
from jax.experimental.pallas import tpu as pltpu
from jax.sharding import PartitionSpec as P

MID = 2
DDEV = 16


def extended_2(block, sides, width):
    for axis, dim in sides:
        count = lax.axis_size(axis)
        forward = [(i, i + 1) for i in range(count - 1)]
        backward = [(target, source) for source, target in forward]
        low = lax.ppermute(
            lax.slice_in_dim(block, block.shape[dim] - width, None, axis=dim), axis, forward
        )
        high = lax.ppermute(lax.slice_in_dim(block, 0, width, axis=dim), axis, backward)
        block = jnp.concatenate([low, block, high], axis=dim)
    return block


def passed_along(x, axis, by):
    peers = lax.axis_size(axis)
    pairs = [(i, i + by) for i in range(peers) if 0 <= i + by < peers]
    return lax.ppermute(x, axis, pairs)


def combined_all(part, axis, combine):
    gathered = jax.tree.map(lambda a: lax.all_gather(a, axis), part)

    def take(source):
        return jax.tree.map(lambda a: lax.dynamic_index_in_dim(a, source, 0, False), gathered)

    return lax.fori_loop(
        1, lax.axis_size(axis), lambda source, state: combine(state, take(source)), take(0)
    )


def correlate(left_full, extended, groups, first_disp, count, total_disp):
    rows_here, width_here, channels = left_full.shape
    group_size = channels // groups
    left_groups = left_full.reshape(rows_here, width_here, groups, group_size)

    def single(offset):
        disp_value = first_disp + offset
        shifted = lax.dynamic_slice_in_dim(extended, 2 * width_here - disp_value, width_here, 1)
        right_groups = shifted.reshape(rows_here, width_here, groups, group_size)
        corr = (
            jnp.einsum(
                "hwgc,hwgc->ghw", left_groups, right_groups, preferred_element_type=jnp.float32
            )
            / group_size
        )
        inside = (disp_value >= 0) & (disp_value < total_disp)
        return jnp.where(inside, corr, 0.0).astype(jnp.bfloat16)

    return lax.map(single, jnp.arange(count, dtype=jnp.int32))


def convolve(padded, kernel):
    depth_out = padded.shape[0] - 2
    in_chans = padded.shape[1]
    rows_out = padded.shape[2] - 2
    cols_out = padded.shape[3] - 2
    out_chans = kernel.shape[1]
    columns = jnp.concatenate(
        [
            padded[:, :, row_tap : row_tap + rows_out, col_tap : col_tap + cols_out]
            for row_tap in range(3)
            for col_tap in range(3)
        ],
        axis=1,
    )
    flat = columns.reshape(depth_out + 2, 9 * in_chans, rows_out * cols_out)
    summed = jnp.zeros((depth_out, out_chans, rows_out * cols_out), jnp.float32)
    for disp_tap in range(3):
        taps = (
            jnp.transpose(kernel[9 * disp_tap : 9 * disp_tap + 9], (1, 0, 2))
            .reshape(out_chans, 9 * in_chans)
            .astype(flat.dtype)
        )
        summed = summed + jnp.einsum(
            "ok,dkn->don",
            taps,
            flat[disp_tap : disp_tap + depth_out],
            preferred_element_type=jnp.float32,
            precision=lax.Precision.HIGHEST,
        )
    return summed.reshape(depth_out, out_chans, rows_out, cols_out)


def widen(hidden):
    return extended_2(hidden, (("disp", 0), ("rows", 2), ("cols", 3)), 1)


def combine_parts(earlier, later):
    highest = jnp.maximum(earlier[0], later[0])
    scale_one = jnp.exp(earlier[0] - highest)
    scale_two = jnp.exp(later[0] - highest)
    return (
        highest,
        earlier[1] * scale_one + later[1] * scale_two,
        earlier[2] * scale_one + later[2] * scale_two,
    )


def shards(left_feat, right_feat, conv_first, conv_mid, conv_last):
    piece_width = left_feat.shape[1]
    groups = conv_first.shape[2]
    disp_count = lax.axis_size("disp")
    depth_here = DDEV
    total_disp = depth_here * disp_count
    first_disp = lax.axis_index("disp") * depth_here
    left_full, right_full = (
        lax.all_gather(left_feat, "disp", axis=1, tiled=True),
        lax.all_gather(right_feat, "disp", axis=1, tiled=True),
    )
    prior_full = passed_along(right_full, "cols", 1)
    extended = jnp.concatenate([jnp.zeros_like(right_full), prior_full, right_full], axis=1)
    volume = correlate(left_full, extended, groups, first_disp, depth_here, total_disp)
    padded = extended_2(volume, (("disp", 0), ("rows", 2), ("cols", 3)), 1)
    hidden = jax.nn.relu(convolve(padded, conv_first))
    for layer in range(MID):
        hidden = jax.nn.relu(convolve(widen(hidden), conv_mid[layer]))
    cost_cube = convolve(widen(hidden), conv_last)[:, 0]
    levels = (
        (first_disp + jnp.arange(depth_here, dtype=jnp.int32)).astype(jnp.float32) / total_disp
    )[:, None, None]
    local_high = jnp.max(cost_cube, axis=0)
    weights = jnp.exp(cost_cube - local_high[None])
    merged = combined_all(
        (local_high, jnp.sum(weights, axis=0), jnp.sum(weights * levels, axis=0)),
        "disp",
        combine_parts,
    )
    whole_row = merged[2] / merged[1]
    return lax.dynamic_slice_in_dim(whole_row, lax.axis_index("disp") * piece_width, piece_width, 1)


HALO = 4
GROUP = 4
EDGE = 8
BLOCK = 8
SLAB = 128


def build_permutation(perm_ref, channels, groups):
    size = channels // groups
    rows, lanes = perm_ref.shape
    part = rows // 2
    lane = lax.broadcasted_iota(jnp.int32, (1, lanes), 1)
    group = lane % 64
    for row in range(2):
        wanted = group * size + lane // SLAB
        wanted = jnp.where((group < groups) & ((lane // 64) % 2 == row), wanted, -1)
        channel = lax.broadcasted_iota(jnp.int32, (part, lanes), 0)
        block = (channel == wanted).astype(jnp.float32).astype(jnp.bfloat16)
        perm_ref[row * part : (row + 1) * part, :] = block


def tap_of(a, r_in, r_out, e):
    return 9 * a + 3 * (r_in - r_out + 1) + e


def place_first(target, at, lead, slabs):
    for a, slab in enumerate(slabs):
        lane = SLAB * (lead + a)
        target[at : at + slab.shape[0], lane : lane + SLAB] = slab


def build_first(taps_ref, pair_ref, quad_ref):
    pair_ref[...] = jnp.zeros_like(pair_ref)
    quad_ref[...] = jnp.zeros_like(quad_ref)
    outs, ins = taps_ref.shape[1:]
    blank = jnp.zeros((outs, 64 - ins), jnp.float32)
    for e in range(3):
        for r_out in range(2):
            slabs = []
            for a in range(3):
                parts = []
                for r_in in range(2):
                    parts += [taps_ref[tap_of(a, r_in, r_out, e)].astype(jnp.float32), blank]
                slabs.append(jnp.concatenate(parts, axis=1).astype(jnp.bfloat16))
            if e < 2:
                for d_out in range(2):
                    place_first(pair_ref, e * 128 + d_out * 64 + r_out * 32, d_out, slabs)
            else:
                for d_out in range(GROUP):
                    place_first(quad_ref, d_out * 64 + r_out * 32, d_out, slabs)


def place_mid(target, at, lead, block):
    for half in range(2):
        piece = block[:, SLAB * half : SLAB * half + SLAB]
        for copy in range(2):
            lane = 2 * SLAB * (lead + half) + SLAB * copy
            target[at : at + piece.shape[0], lane : lane + SLAB] = piece


def build_mid(taps_ref, pair_ref, quad_ref):
    pair_ref[...] = jnp.zeros_like(pair_ref)
    quad_ref[...] = jnp.zeros_like(quad_ref)
    outs = taps_ref.shape[1]
    blank = jnp.zeros((outs, 64), jnp.float32)
    for e in range(3):
        for r_out in range(2):
            slabs = [
                taps_ref[tap_of(a, r_in, r_out, e)].astype(jnp.float32)
                for a in range(3)
                for r_in in range(2)
            ]
            shifted = (
                jnp.concatenate(slabs + [blank], axis=1).astype(jnp.bfloat16),
                jnp.concatenate([blank] + slabs, axis=1).astype(jnp.bfloat16),
            )
            if e < 2:
                for d_out in range(2):
                    place_mid(pair_ref, e * 128 + d_out * 64 + r_out * 32, 0, shifted[d_out])
            else:
                for d_out in range(GROUP):
                    place_mid(
                        quad_ref, d_out * 64 + r_out * 32, d_out // 2, shifted[d_out % 2]
                    )


def build_last(taps_ref, line_ref, row):
    taps = taps_ref[...].astype(jnp.float32)
    lines = []
    for e in range(3):
        for d_out in range(GROUP):
            parts = []
            for a in range(3):
                for r_in in range(2):
                    upper, lower = (tap_of(a, r_in, r_out, e) for r_out in range(2))
                    parts.append(
                        jnp.where(row == 0, taps[upper : upper + 1], taps[lower : lower + 1])
                    )
            if d_out > 0:
                parts.insert(0, jnp.zeros((1, 64 * d_out), jnp.float32))
            if d_out < GROUP - 1:
                parts.append(jnp.zeros((1, 64 * (GROUP - 1 - d_out)), jnp.float32))
            lines.append(jnp.concatenate(parts, axis=1))
        lines.append(jnp.zeros((8 - GROUP, 3 * SLAB), jnp.float32))
    lines.append(jnp.zeros((8, 3 * SLAB), jnp.float32))
    block = jnp.concatenate(lines, axis=0).astype(jnp.bfloat16)
    for pair in range(3):
        piece = block[:, SLAB * pair : SLAB * pair + SLAB]
        for copy in range(2):
            lane = SLAB * (2 * pair + copy)
            line_ref[:, lane : lane + SLAB] = piece


def across(x, banded):
    return lax.dot_general(
        x, banded, (((1,), (1,)), ((), ())), preferred_element_type=jnp.float32
    )


def exchange_plan(width):
    n = width // BLOCK
    near = [(-1, other, None, 3 * n + 1, 2) for other in (1, 0)]
    near.append((0, 1, 0, 0, 2 * n))
    near += [(1, other, n - 1, 2 * n, n + 1) for other in (1, 0)]
    far = [(2, other, n, 3 * n + 3, n) for other in (1, 0)]
    far += [(3, other, 2 * n - 1, 4 * n + 3, 1) for other in (1, 0)]
    right, left = n + n + 1, 3 * n + 3
    places = (
        (0, n, left),
        (n, n, right),
        (2 * n, 1, left - 1),
        (2 * n + 1, n, right - n),
        (3 * n + 1, 1, right + n),
        (3 * n + 2, 1, left + n),
        (3 * n + 3, n, right - 2 * n),
        (4 * n + 3, 1, 0),
    )
    own, left_at = right * BLOCK, (left - 1) * BLOCK
    return tuple(near), tuple(far), places, own, left_at, (4 * n + 4) * BLOCK


def exchange_steps(left_ref, right_ref, held, edge_ref, send_sem, recv_sem, own_sem, told_sem):
    width = left_ref.shape[0] * BLOCK
    blocks = width // BLOCK
    near, far, _, _, _, _ = exchange_plan(width)
    copies = near + far
    row, col, disp = lax.axis_index("rows"), lax.axis_index("cols"), lax.axis_index("disp")
    col_disps = lax.axis_size("disp")
    pieces = col_disps * lax.axis_size("cols")
    piece = col * col_disps + disp
    barrier = pltpu.get_barrier_semaphore()
    reach = max(abs(by) for by, _, _, _, _ in copies)
    steps = sorted({by for by, _, _, _, _ in copies if by})
    related = [by for by in range(-reach, reach + 1) if by]

    def device(other, by):
        target = piece + by
        target_col = (target >= col_disps).astype(jnp.int32)
        return {
            "tiles": lax.axis_index("tiles"),
            "disp": target - col_disps * target_col,
            "rows": 1 - row if other else row,
            "cols": target_col,
        }

    def exists(by):
        return (piece + by >= 0) & (piece + by < pieces)

    def stays(by):
        return (disp + by >= 0) & (disp + by < col_disps)

    def lower(by):
        return stays(by) if by < 0 else exists(by) & (disp + by >= col_disps)

    def higher(by):
        return stays(by) if by > 0 else exists(by) & (disp + by < 0)

    def copy(number):
        by, other, source, target, count = copies[number]
        return pltpu.make_async_remote_copy(
            src_ref=edge_ref if source is None else held.at[row, pl.ds(source, count)],
            dst_ref=held.at[row, pl.ds(target, count)],
            send_sem=send_sem.at[number],
            recv_sem=recv_sem.at[number],
            device_id=device(other, by),
            device_id_type=pl.DeviceIdType.MESH,
        )

    own_loads = [
        pltpu.make_async_copy(source, held.at[row, pl.ds(target, blocks)], own_sem.at[number])
        for number, (source, target) in enumerate(((left_ref, 0), (right_ref, blocks)))
    ]

    def tell(semaphore, by, other):
        pl.semaphore_signal(
            semaphore, inc=1, device_id=device(other, by), device_id_type=pl.DeviceIdType.MESH
        )

    def greet():
        for load in own_loads:
            load.start()
        empty = (2, held.shape[1] - 2 * blocks, BLOCK, held.shape[3])
        held[:, 2 * blocks :] = jnp.zeros(empty, held.dtype)
        tell(barrier, 0, 1)
        for by in related:

            @pl.when(higher(by))
            def _():
                for other in range(2):
                    tell(barrier, by, other)

    def start(by):
        for number, (step, _, _, _, _) in enumerate(copies):
            if step == by:
                copy(number).start()

    def meet():
        count = jnp.int32(1)
        for by in related:
            count = count + 2 * lower(by).astype(jnp.int32)
        pl.semaphore_wait(barrier, count)
        for by in steps:

            @pl.when(lower(-by))
            def _():
                for other in range(2):
                    tell(told_sem.at[steps.index(by)], -by, other)

        for load in own_loads:
            load.wait()
        edge_ref[0] = held[row, blocks]
        edge_ref[1] = held[row, 0]

    def send(by):
        if by == 0:
            start(by)
        else:

            @pl.when(lower(by))
            def _():
                start(by)

    def send_told(by):
        @pl.when(higher(by))
        def _():
            pl.semaphore_wait(told_sem.at[steps.index(by)], 2)
            start(by)

    def receive(numbers):
        for number in numbers:

            @pl.when(exists(-copies[number][0]))
            def _():
                copy(number).wait_recv()

    def receive_near():
        receive(range(len(near)))

    def receive_far():
        receive(range(len(near), len(copies)))

    def finish():
        for number in range(len(copies)):

            @pl.when(exists(copies[number][0]))
            def _():
                copy(number).wait_send()

    return greet, meet, send, send_told, receive_near, receive_far, finish


def whole_kernel(
    disps,
    width_all,
    left_ref,
    right_ref,
    first_hbm,
    mid_hbm,
    last_hbm,
    out_ref,
    feat_ref,
    edge_ref,
    send_sem,
    recv_sem,
    own_sem,
    told_sem,
    load_sem,
    perm_ref,
    first_taps,
    mid_taps,
    last_taps,
    a_ref,
    p_ref,
    f_ref,
    pair_ref,
    quad_ref,
    line_ref,
    kpair_ref,
    kquad_ref,
):
    width_here = out_ref.shape[1]
    wide = width_here + 2 * HALO
    groups_d = disps // GROUP + 1
    channels, groups = left_ref.shape[2], first_taps.shape[2]
    size = channels // groups
    _, _, places, own, left_at, held_rows = exchange_plan(width_here)
    greet, meet, send, send_told, receive_near, receive_far, finish = exchange_steps(
        left_ref, right_ref, feat_ref, edge_ref, send_sem, recv_sem, own_sem, told_sem
    )
    loads = [
        pltpu.make_async_copy(source, target, load_sem.at[number])
        for number, (source, target) in enumerate(
            ((first_hbm, first_taps), (mid_hbm, mid_taps), (last_hbm, last_taps))
        )
    ]
    greet()
    for load in loads:
        load.start()
    meet()
    for by in (1, 0, 2, 3, -1):
        send(by)
    build_permutation(perm_ref, channels, groups)
    send_told(1)
    a_ref[0, 0:wide, :] = jnp.zeros((wide, 6 * SLAB), jnp.bfloat16)
    for layer in range(MID + 2):
        a_ref[layer, (groups_d - 1) * wide : groups_d * wide, 4 * SLAB :] = jnp.zeros(
            (wide, 2 * SLAB), jnp.bfloat16
        )
    loads[0].wait()
    build_first(first_taps, pair_ref.at[0], quad_ref.at[0])
    send_told(2)
    loads[1].wait()
    for layer in range(MID):
        build_mid(mid_taps.at[layer], pair_ref.at[layer + 1], quad_ref.at[layer + 1])
    loads[2].wait()
    for layer in range(MID + 1):
        kpair_ref[layer] = pair_ref[layer].T
        kquad_ref[layer] = quad_ref[layer].T
    build_last(last_taps, line_ref, lax.axis_index("rows"))

    def permute(start, stop):
        held = [
            feat_ref[row, start // BLOCK : stop // BLOCK].reshape(stop - start, channels)
            for row in range(2)
        ]
        for at in range(0, size * SLAB, 2 * SLAB):
            lanes = slice(at, at + 2 * SLAB)
            both = jnp.dot(
                held[0],
                perm_ref[0:channels, lanes],
                preferred_element_type=jnp.float32,
            ) + jnp.dot(
                held[1],
                perm_ref[channels : 2 * channels, lanes],
                preferred_element_type=jnp.float32,
            )
            for first, count, place in places:
                begin, end, to = (BLOCK * x for x in (first, first + count, place))
                if start <= begin < stop:
                    rows, held_to = slice(begin - start, end - start), slice(to, to + end - begin)
                    f_ref[at // SLAB, held_to] = both[rows, :SLAB]
                    f_ref[at // SLAB + 1, held_to] = both[rows, SLAB:]

    def volume(start, stop):
        for group in range(start, stop):
            sums = [None] * GROUP
            for k in range(size):
                left = f_ref[k, left_at + EDGE - HALO : left_at + EDGE - HALO + wide]
                for place in range(GROUP):
                    at = own - HALO - (GROUP * (group - 1) + place)
                    term = left * f_ref[k, at : at + wide]
                    sums[place] = term if k == 0 else sums[place] + term
            for place in range(GROUP):
                slab = (sums[place] / size).astype(jnp.bfloat16)
                here = slice(group * wide, (group + 1) * wide)
                a_ref[0, here, SLAB * place : SLAB * place + SLAB] = slab
                if place < 2:
                    before = slice((group - 1) * wide, group * wide)
                    lane = SLAB * (GROUP + place)
                    a_ref[0, before, lane : lane + SLAB] = slab

    piece = lax.axis_index("cols") * lax.axis_size("disp") + lax.axis_index("disp")
    column = piece * width_here - HALO + lax.broadcasted_iota(jnp.int32, (wide, SLAB), 0)
    in_image = (column >= 0) & (column < width_all)
    lane_disp = lax.broadcasted_iota(jnp.int32, (wide, SLAB), 1) // 64

    def products(layer, start, stop):
        source, part = a_ref.at[layer], p_ref.at[layer]
        middle = (start + stop) // 2

        def multiply(slab, first, last, lanes, taps_ref):
            rows = slice(first * wide, last * wide)
            got = jnp.dot(source[rows, lanes], taps_ref[layer], preferred_element_type=jnp.float32)
            held = slice(8 + first * wide, 8 + last * wide)
            part[slab, held] = got[:, :SLAB]
            part[slab + 1, held] = got[:, SLAB:]

        multiply(0, start, stop, slice(0, 4 * SLAB), kpair_ref)
        multiply(2, start, stop, slice(2 * SLAB, 6 * SLAB), kpair_ref)
        multiply(4, start, middle, slice(0, 6 * SLAB), kquad_ref)
        multiply(4, middle, stop, slice(0, 6 * SLAB), kquad_ref)

    def finish_layer(layer, start, stop):
        target, part = a_ref.at[layer + 1], p_ref.at[layer]
        base = layer + 1 - HALO
        for group in range(start, stop):
            at = 8 + group * wide
            here = slice(group * wide, (group + 1) * wide)
            before = slice((group - 1) * wide, group * wide)
            for half in range(2):
                total = (
                    part[2 * half, at - 1 : at - 1 + wide]
                    + part[2 * half + 1, at : at + wide]
                    + part[4 + half, at + 1 : at + 1 + wide]
                )
                low = base + GROUP * group + 2 * half
                keep = in_image
                if low < 0 or low + 2 > disps:
                    keep = keep & (lane_disp >= -low) & (lane_disp < disps - low)
                total = jnp.where(keep, jnp.maximum(total, 0.0), 0.0)
                high = total.astype(jnp.bfloat16)
                rest = (total - high.astype(jnp.float32)).astype(jnp.bfloat16)
                lane = 2 * SLAB * half
                target[here, lane : lane + SLAB] = high
                target[here, lane + SLAB : lane + 2 * SLAB] = rest
                if half == 0 and group > 0:
                    target[before, 4 * SLAB : 5 * SLAB] = high
                    target[before, 5 * SLAB : 6 * SLAB] = rest

    send_told(3)
    send_told(-1)
    near_rows = held_rows - width_here - BLOCK
    receive_near()
    permute(0, near_rows)
    volume(1, 8)
    receive_far()
    permute(near_rows, held_rows)
    volume(8, groups_d)
    waiting = []

    def step(layer, start, stop):
        products(layer, start, stop)
        if waiting:
            finish_layer(*waiting.pop())
        waiting.append((layer, start, stop))

    for layer, bounds in enumerate(((0, 9, groups_d), (0, 8, groups_d), (0, 7, groups_d))):
        for start, stop in zip(bounds, bounds[1:]):
            step(layer, start, stop)

    per = SLAB // wide
    lane = lax.broadcasted_iota(jnp.int32, (8, SLAB), 1)
    place = lax.broadcasted_iota(jnp.int32, (8, SLAB), 0)
    within = (lane + HALO) // wide
    firsts = list(range(0, groups_d - 1, per))
    lowest = jnp.finfo(jnp.float32).min
    costs = []
    valids = []
    for begin in range(0, len(firsts), 2):
        some = firsts[begin : begin + 2]
        if waiting and some[-1] + per >= waiting[0][1]:
            finish_layer(*waiting.pop())
        taken = [a_ref[MID + 1, first * wide : first * wide + SLAB] for first in some]
        joined = across(line_ref[...], jnp.concatenate(taken, axis=0))
        for number, first in enumerate(some):
            parts = joined[:, SLAB * number : SLAB * number + SLAB]
            cost = (
                pltpu.roll(parts[0:8], SLAB + 1 - HALO, 1)
                + pltpu.roll(parts[8:16], SLAB - HALO, 1)
                + pltpu.roll(parts[16:24], SLAB - 1 - HALO, 1)
            )
            valid = (place < GROUP) & (within < min(per, groups_d - 1 - first))
            valids.append(valid)
            costs.append(jnp.where(valid, cost, lowest))
    tops = functools.reduce(jnp.maximum, costs)
    weight_sum = jnp.zeros((8, SLAB), jnp.float32)
    level_sum = jnp.zeros((8, SLAB), jnp.float32)
    for number, cost in enumerate(costs):
        weight = jnp.where(valids[number], jnp.exp(cost - tops), 0.0)
        level = GROUP * (number * per + within) + place
        weight_sum += weight
        level_sum += weight * (level.astype(jnp.float32) * (1.0 / disps))

    def spread(x):
        return [x] + [pltpu.roll(x, SLAB - wide * k, 1) for k in range(1, per)]

    def merged(scales, x):
        return functools.reduce(jnp.add, [a * b for a, b in zip(scales, spread(x))])

    top = jnp.broadcast_to(jnp.max(tops, axis=0, keepdims=True), (8, SLAB))
    scale = jnp.exp(tops - top)
    weight_sum = jnp.broadcast_to(jnp.sum(weight_sum * scale, axis=0, keepdims=True), (8, SLAB))
    level_sum = jnp.broadcast_to(jnp.sum(level_sum * scale, axis=0, keepdims=True), (8, SLAB))
    around = spread(top)
    highest = functools.reduce(jnp.maximum, around)
    scales = [jnp.exp(one - highest) for one in around]
    line = merged(scales, level_sum) / merged(scales, weight_sum)
    out_ref[...] = line[0:1, 0:width_here]
    finish()


def window_shards(left_feat, right_feat, conv_first, conv_mid, conv_last):
    width = left_feat.shape[1]
    channels = left_feat.shape[2]
    groups = conv_first.shape[2]
    disps = DDEV * lax.axis_size("disp")
    width_all = width * lax.axis_size("disp") * lax.axis_size("cols")
    near, far, _, _, _, held_rows = exchange_plan(width)
    count = len(near) + len(far)
    wide = width + 2 * HALO
    rows = (disps // GROUP + 1) * wide
    size = channels // groups
    return pl.pallas_call(
        functools.partial(whole_kernel, disps, width_all),
        out_shape=pltpu.VMEM((1, width), jnp.float32),
        in_specs=[pl.BlockSpec(memory_space=pltpu.HBM)] * 5,
        out_specs=pl.BlockSpec(memory_space=pltpu.VMEM),
        scratch_shapes=[
            pltpu.VMEM((2, held_rows // BLOCK, BLOCK, channels), jnp.bfloat16),
            pltpu.VMEM((2, BLOCK, channels), jnp.bfloat16),
            pltpu.SemaphoreType.DMA((count,)),
            pltpu.SemaphoreType.DMA((count,)),
            pltpu.SemaphoreType.DMA((2,)),
            pltpu.SemaphoreType.REGULAR((4,)),
            pltpu.SemaphoreType.DMA((3,)),
            pltpu.VMEM((2 * channels, size * SLAB), jnp.bfloat16),
            pltpu.VMEM(conv_first.shape, jnp.bfloat16),
            pltpu.VMEM(conv_mid.shape, jnp.bfloat16),
            pltpu.VMEM((27, conv_last.shape[2]), jnp.bfloat16),
            pltpu.VMEM((MID + 2, rows + 2 * wide, 6 * SLAB), jnp.bfloat16),
            pltpu.VMEM((MID + 1, 6, rows + 16, SLAB), jnp.float32),
            pltpu.VMEM((size, held_rows, SLAB), jnp.float32),
            pltpu.VMEM((MID + 1, 2 * SLAB, 4 * SLAB), jnp.bfloat16),
            pltpu.VMEM((MID + 1, 2 * SLAB, 6 * SLAB), jnp.bfloat16),
            pltpu.VMEM((32, 6 * SLAB), jnp.bfloat16),
            pltpu.VMEM((MID + 1, 4 * SLAB, 2 * SLAB), jnp.bfloat16),
            pltpu.VMEM((MID + 1, 6 * SLAB, 2 * SLAB), jnp.bfloat16),
        ],
        compiler_params=pltpu.CompilerParams(
            vmem_limit_bytes=56 * 1024 * 1024, collective_id=0, has_side_effects=True
        ),
    )(
        left_feat.reshape(-1, BLOCK, channels),
        right_feat.reshape(-1, BLOCK, channels),
        conv_first,
        conv_mid,
        conv_last.reshape(27, -1),
    )


def solution(mesh):
    rows, pieces = mesh.shape["rows"], mesh.shape["cols"] * mesh.shape["disp"]
    body = window_shards if rows == 2 and mesh.shape["disp"] == 4 and pieces == 8 else shards
    return jax.shard_map(
        body,
        mesh=mesh,
        in_specs=(
            P(("tiles", "rows"), ("cols", "disp"), None),
            P(("tiles", "rows"), ("cols", "disp"), None),
            P(),
            P(),
            P(),
        ),
        out_specs=P(("tiles", "rows"), ("cols", "disp")),
        check_vma=False,
    )
```
